32 devices in a mesh: section: 2 (over core), row: 4 (over z), col: 4 (over y, x).
Axes of the slice: x: 2, y: 2, z: 4, core: 2. Of those that a mesh axis runs over, the one named last changes fastest.
Arguments:
- queries: bfloat16 [16384, 4096], P(('section', 'col'), 'row'), may hold values from -8 to 8
- keys: bfloat16 [16384, 512], P(('section', 'col')), may hold values from -6 to 6
- values: bfloat16 [16384, 512], P(('section', 'col')), may hold values from -6 to 6
- out_grad: bfloat16 [16384, 4096], P(('section', 'col'), 'row'), may hold values from -12 to 12
- q_weight: bfloat16 [2048, 4096], P('col', 'row'), may hold values from -0.125 to 0.125
- k_weight: bfloat16 [2048, 512], P('col'), may hold values from -0.125 to 0.125
- v_weight: bfloat16 [2048, 512], P('col'), may hold values from -0.125 to 0.125
- resid_grad: bfloat16 [16384, 2048], P(('section', 'row', 'col')), may hold values from -4 to 4
- moe_input: bfloat16 [16384, 2048], P(('section', 'row', 'col')), may hold values from -6 to 6
- expert_ids: int32 [16384, 8], P(('section', 'row', 'col')), may hold values from 0 to 31, all different within a row; in each aligned block of 512 rows (0 to 511, 512 to 1023, ...) at most 144 rows name the same one
- route_weights: float32 [16384, 8], P(('section', 'row', 'col')), may hold values from 0.03 to 0.4
- w_gate_up: bfloat16 [32, 2048, 1536], P(('section', 'row', 'col')), may hold values from -0.125 to 0.125
- w_down: bfloat16 [32, 768, 2048], P(('section', 'row', 'col')), may hold values from -0.21875 to 0.21875
Outputs:
- moe_input_grad: bfloat16 [16384, 2048], P(('section', 'row', 'col'))
The draws below stay inside these ranges and needn't reach their ends.
Inputs may be any that keep to these rules, and one draw needn't show every extreme that they name: `expert_ids`: each row names 8 different experts; among the rows of one device no expert is named by more than 144 rows, and in every draw some expert is named by exactly 144 rows of some device.
All inputs are finite; a program needn't handle non-finite values.
Results may differ from the reference program's by a relative error of at most 0.02.
Values may be sent and summed in bfloat16 or wider, within the bound.
A program may use at most 256 MiB of HBM per device.

```python
import math
import jax
import jax.numpy as jnp
import numpy as np
from jax import lax

D = 2048
HEADS = 32
KV_HEADS = 4
HEAD_DIM = 128
EXP_FF = 768
TOPK = 8
DOC = 1024
EXPERTS = 32
TOK_MOE = 512
TOKENS = 16384
HQ_DEV = 8
CAP = 144
N_ROW = 4
N_COL = 4


def draw_keys(key, part):
    shape = (TOKENS, KV_HEADS * HEAD_DIM)
    base = jnp.clip(jax.random.normal(jax.random.fold_in(key, 11), shape, jnp.float32), -6.0, 6.0)
    return base.astype(jnp.bfloat16)


def draw_queries(key, part):
    shape = (TOKENS, HEADS * HEAD_DIM)
    base = jnp.clip(jax.random.normal(jax.random.fold_in(key, 21), shape, jnp.float32), -6.0, 6.0)
    return base.astype(jnp.bfloat16)


def level_of(own_key, shape, pieces, least, high):
    factor_of, own = 1.0, jax.random.fold_in(own_key, 6)
    for dim, blocks in pieces:
        draws = jnp.exp(jax.random.uniform(jax.random.fold_in(own, dim), (blocks,), jnp.float32, least / len(pieces), high / len(pieces)))
        factor_of = factor_of * jnp.repeat(draws, shape[dim] // blocks).reshape([-1 if axis == dim else 1 for axis in range(len(shape))])
    return factor_of


def assign_block(key, own, number, rows, amount, top, most, slope):
    ranking = jax.random.permutation(key, amount)
    heavy_load, ordinary = shares(amount, rows * top, most, slope, True), shares(amount, rows * top, most, slope, False)
    places = jnp.arange(amount)

    def named(sizes, offset_by):
        used = int((sizes > 0).sum())
        fixed = max(1, used // 4)
        moved = fixed + (places - fixed + offset_by * (used - fixed)) % max(1, amount - fixed)
        return jnp.zeros((amount,), jnp.int32).at[ranking[jnp.where(places < fixed, places, moved)]].set(jnp.asarray(sizes, jnp.int32))

    sizes = jnp.where(number % 4 == 0, named(heavy_load, number // 4), named(ordinary, number - number // 4 - 1))
    mixed = jax.random.permutation(jax.random.fold_in(own, 3), amount)
    giver, sink = mixed[0:amount // 2 * 2:2], mixed[1:amount // 2 * 2:2]
    margin = jnp.minimum(sizes[giver] - 1, most - sizes[sink]) // 2
    margin = jnp.where((giver == ranking[0]) | (sink == ranking[0]) | (sizes[sink] == 0), 0, jnp.maximum(margin, 0))
    moved = jax.random.randint(jax.random.fold_in(own, 4), (amount // 2,), 0, 1 << 20) % (margin + 1)
    sizes = sizes.at[giver].add(-moved).at[sink].add(moved)
    items = jnp.searchsorted(jnp.cumsum(sizes), jnp.arange(rows * top), side="right").astype(jnp.int32)
    grid = items.reshape(top, rows).T
    grid = grid[jax.random.permutation(jax.random.fold_in(own, 1), rows)]
    offset_by = jax.random.randint(jax.random.fold_in(own, 2), (rows, 1), 0, top)
    return jnp.take_along_axis(grid, (jnp.arange(top)[None, :] + offset_by) % top, axis=1)


def shares(number_of, total, most, skew, full):
    portions = [(1 << 20) // math.isqrt(rank ** skew) + 1 for rank in range(1, number_of + 1)]
    largest = most if full else min(most, max(-(-total // number_of), total * portions[0] // sum(portions)))
    least = 1 if total - largest >= number_of - 1 else 0
    counts, spare = [largest] + [least] * (number_of - 1), total - largest - least * (number_of - 1)
    while spare > 0:
        movable = [i for i in range(1, number_of) if counts[i] < largest] or [i for i in range(1, number_of) if counts[i] < most]
        whole, left = sum([portions[i] for i in movable]), spare
        for i in movable:
            extra = min(most - counts[i], max(1, left * portions[i] // whole), spare)
            counts[i] = counts[i] + extra
            spare = spare - extra
    return np.array(counts)


def scatter_about(rng, extent, scale, most, cuts=(), held_as=jnp.bfloat16):
    values = jax.random.normal(rng, extent, jnp.float32) * scale
    if len(cuts) > 0:
        values = level_of(rng, extent, cuts, -0.22, 0.18) * values
    return jnp.clip(values, min=-most, max=most).astype(held_as)


def setup_inputs(seed: int = 0) -> dict:
    seeds = jax.random.split(jax.random.key(seed), 14)
    queries = draw_queries(jax.random.fold_in(seeds[13], 71), 0)
    keys = draw_keys(jax.random.fold_in(seeds[13], 71), 0)
    values = scatter_about(seeds[2], (TOKENS, KV_HEADS * HEAD_DIM), 1.0, 6.0, ((0, 8),))
    out_grad = scatter_about(seeds[3], (TOKENS, HEADS * HEAD_DIM), 2.0, 12.0, ((0, 8), (1, 4)))
    q_weight = scatter_about(seeds[4], (D, HEADS * HEAD_DIM), D ** -0.5, 0.125, ((0, 4), (1, 4)))
    k_weight = scatter_about(seeds[5], (D, KV_HEADS * HEAD_DIM), D ** -0.5, 0.125, ((0, 4),))
    v_weight = scatter_about(seeds[6], (D, KV_HEADS * HEAD_DIM), D ** -0.5, 0.125, ((0, 4),))
    resid_grad = scatter_about(seeds[7], (TOKENS, D), 0.5, 4.0, ((0, 32),))
    moe_input = scatter_about(seeds[8], (TOKENS, D), 1.0, 6.0, ((0, 32),))
    expert_ids_keys = jax.random.split(jax.random.fold_in(seeds[9], 1), TOKENS // TOK_MOE)
    expert_ids_turns = jax.random.permutation(jax.random.fold_in(seeds[9], 3), TOKENS // TOK_MOE)
    expert_ids = jax.vmap(lambda own, number: assign_block(jax.random.fold_in(seeds[9], 2), own, number, TOK_MOE, EXPERTS, TOPK, CAP, 2))(expert_ids_keys, expert_ids_turns).reshape((TOKENS, TOPK))
    route_weights = jnp.clip(jnp.exp(math.log(0.4) - 2.5902672 * jax.random.uniform(seeds[10], (TOKENS, TOPK), jnp.float32) ** level_of(seeds[10], (TOKENS, TOPK), ((0, 32),), -0.2, 0.2)), 0.03, 0.4)
    w_gate_up = scatter_about(seeds[11], (EXPERTS, D, 2 * EXP_FF), D ** -0.5, 0.125, ((0, 32),))
    w_down = scatter_about(seeds[12], (EXPERTS, EXP_FF, D), EXP_FF ** -0.5, 0.21875, ((0, 32),))
    return {"queries": queries, "keys": keys, "values": values, "out_grad": out_grad, "q_weight": q_weight, "k_weight": k_weight, "v_weight": v_weight, "resid_grad": resid_grad, "moe_input": moe_input, "expert_ids": expert_ids, "route_weights": route_weights, "w_gate_up": w_gate_up, "w_down": w_down}


def expert_math(rows_in, grad_in, w_gu, w_dn):
    width = w_dn.shape[0]
    gate_up = jnp.dot(rows_in, w_gu, preferred_element_type=jnp.float32)
    gate = gate_up[:, :width]
    up_part = gate_up[:, width:]
    dhidden = lax.dot_general(grad_in, w_dn, (((1,), (1,)), ((), ())), preferred_element_type=jnp.float32)
    sigm = jax.nn.sigmoid(gate)
    d_gate = dhidden * up_part * sigm * (1.0 + gate * (1.0 - sigm))
    d_up = dhidden * gate * sigm
    dgate_up = jnp.concatenate([d_gate, d_up], axis=1).astype(jnp.bfloat16)
    back_rows = lax.dot_general(dgate_up, w_gu, (((1,), (1,)), ((), ())), preferred_element_type=jnp.float32)
    return back_rows.astype(jnp.bfloat16)


def reference(queries, keys, values, out_grad, q_weight, k_weight, v_weight, resid_grad, moe_input, expert_ids, route_weights, w_gate_up, w_down):
    group_size = HEADS // KV_HEADS
    num_docs = TOKENS // DOC
    section_total = TOKENS // (N_ROW * N_COL * TOK_MOE)
    scale_val = HEAD_DIM ** -0.5
    qd = queries.reshape(num_docs, DOC, HEADS, HEAD_DIM)
    od = out_grad.reshape(num_docs, DOC, HEADS, HEAD_DIM)
    kd = keys.reshape(num_docs, DOC, KV_HEADS, HEAD_DIM)
    vd = values.reshape(num_docs, DOC, KV_HEADS, HEAD_DIM)
    kv_of_group = (jnp.arange(N_ROW) * HQ_DEV) // group_size
    wq_groups = jnp.transpose(q_weight.reshape(D, N_ROW, HQ_DEV * HEAD_DIM), (1, 0, 2))
    wk_groups = jnp.transpose(k_weight.reshape(D, KV_HEADS, HEAD_DIM)[:, kv_of_group], (1, 0, 2))
    wv_groups = jnp.transpose(v_weight.reshape(D, KV_HEADS, HEAD_DIM)[:, kv_of_group], (1, 0, 2))
    wcat_groups = jnp.concatenate([wq_groups, wk_groups, wv_groups], axis=2).astype(jnp.float32)
    causal = jnp.arange(DOC)[:, None] >= jnp.arange(DOC)[None, :]

    def one_doc(block):
        query_blk, grad_blk, key_blk, value_blk = block
        key_rep = jnp.repeat(key_blk, group_size, axis=1).astype(jnp.float32)
        value_rep = jnp.repeat(value_blk, group_size, axis=1).astype(jnp.float32)
        query_f = query_blk.astype(jnp.float32)
        grad_f = grad_blk.astype(jnp.float32)
        scores = jnp.einsum('qhd,khd->hqk', query_f, key_rep) * scale_val
        scores = jnp.where(causal[None], scores, -jnp.inf)
        top = jnp.max(scores, axis=-1, keepdims=True)
        expo = jnp.exp(scores - top)
        probs = expo / jnp.sum(expo, axis=-1, keepdims=True)
        probs_b = probs.astype(jnp.bfloat16)
        dprob = jnp.einsum('qhd,khd->hqk', grad_f, value_rep)
        delta = jnp.sum(probs * dprob, axis=-1, keepdims=True)
        dscore = (probs * (dprob - delta)).astype(jnp.bfloat16)
        dscore_f = dscore.astype(jnp.float32)
        dquery = (jnp.einsum('hqk,khd->qhd', dscore_f, key_rep) * scale_val).astype(jnp.bfloat16)
        dscore_g = dscore_f.reshape(N_ROW, HQ_DEV, DOC, DOC)
        probs_g = probs_b.astype(jnp.float32).reshape(N_ROW, HQ_DEV, DOC, DOC)
        query_g = query_f.reshape(DOC, N_ROW, HQ_DEV, HEAD_DIM)
        grad_g = grad_f.reshape(DOC, N_ROW, HQ_DEV, HEAD_DIM)
        dkey = (jnp.einsum('ghqk,qghd->gkd', dscore_g, query_g) * scale_val).astype(jnp.bfloat16)
        dvalue = jnp.einsum('ghqk,qghd->gkd', probs_g, grad_g).astype(jnp.bfloat16)
        dquery_g = jnp.transpose(dquery.reshape(DOC, N_ROW, HQ_DEV * HEAD_DIM), (1, 0, 2))
        dqkv = jnp.concatenate([dquery_g, dkey, dvalue], axis=2).astype(jnp.float32)
        part = jnp.einsum('gtc,gdc->gtd', dqkv, wcat_groups)
        part = lax.optimization_barrier(part.astype(jnp.bfloat16)).astype(jnp.float32)
        return jnp.sum(part, axis=0)

    head_grad = lax.map(one_doc, (qd, od, kd, vd))
    head_grad = head_grad.reshape(section_total, N_COL, N_ROW, TOK_MOE, D)
    head_grad = jnp.transpose(head_grad, (0, 2, 1, 3, 4)).reshape(TOKENS, D)
    layer_grad = head_grad + resid_grad.astype(jnp.float32)
    row_grad = layer_grad.astype(jnp.bfloat16)

    limit = EXPERTS * CAP
    rows_pad = jnp.concatenate([moe_input, jnp.zeros((1, D), jnp.bfloat16)], axis=0)
    grads_pad = jnp.concatenate([row_grad, jnp.zeros((1, D), jnp.bfloat16)], axis=0)

    def per_expert(carry, expert):
        hits = expert_ids == expert
        weight = jnp.sum(jnp.where(hits, route_weights, jnp.zeros_like(route_weights)), axis=1)
        weight_pad = jnp.concatenate([weight, jnp.zeros((1,), weight.dtype)], axis=0)
        chosen = jnp.any(hits, axis=1)
        index_list = jnp.nonzero(chosen, size=limit, fill_value=TOKENS)[0].astype(jnp.int32)
        result = expert_math(rows_pad[index_list], grads_pad[index_list], w_gate_up[expert], w_down[expert])
        carry = carry.at[index_list].add(weight_pad[index_list][:, None] * result.astype(jnp.float32))
        return carry, None

    start = jnp.zeros((TOKENS + 1, D), jnp.float32)
    total, unused = lax.scan(per_expert, start, jnp.arange(EXPERTS, dtype=jnp.int32))
    return total[:TOKENS].astype(jnp.bfloat16)
```

```python
import jax
import jax.numpy as jnp
from jax import lax
from jax.experimental import pallas as pl
from jax.experimental.pallas import tpu as pltpu
from jax.sharding import PartitionSpec as P

HEADS = 32
KV_HEADS = 4
HEAD_DIM = 128
TOPK = 8
DOC = 1024
CHUNKS = 2
PART = 512
ATT_BLOCK = 256
LOG2_E = 1.4426950408889634


def slot_hits(pos, cap):
    slot = lax.broadcasted_iota(jnp.int32, (cap, pos.shape[1]), 0)
    return slot == pos


def pick_kernel(pos_ref, rows_ref, out_ref):
    peers, _, cap, width = out_ref.shape
    picks = [
        jnp.where(slot_hits(pos_ref[p, 0], cap), 1.0, 0.0).astype(jnp.bfloat16)
        for p in range(peers)
    ]
    if cap % 16 == 0:
        picked = jnp.dot(
            jnp.concatenate(picks, axis=0), rows_ref[0], preferred_element_type=jnp.float32
        ).astype(out_ref.dtype)
        out_ref[:, 0] = picked.reshape(peers, cap, width)
    else:
        for p in range(peers):
            picked = jnp.dot(picks[p], rows_ref[0], preferred_element_type=jnp.float32)
            out_ref[p, 0] = picked.astype(out_ref.dtype)


def pick_rows(pos, rows, cap):
    peers, groups, _, tokens = pos.shape
    width = rows.shape[2]
    part = min(PART, width)
    return pl.pallas_call(
        pick_kernel,
        grid=(groups, width // part),
        in_specs=[
            pl.BlockSpec((peers, 1, 1, tokens), lambda g, w: (0, g, 0, 0)),
            pl.BlockSpec((1, tokens, part), lambda g, w: (g, 0, w)),
        ],
        out_specs=pl.BlockSpec((peers, 1, cap, part), lambda g, w: (0, g, 0, w)),
        out_shape=jax.ShapeDtypeStruct((peers, groups, cap, width), rows.dtype),
        cost_estimate=pl.CostEstimate(
            flops=2 * peers * groups * cap * tokens * width,
            bytes_accessed=2 * width * groups * (tokens + peers * cap),
            transcendentals=0,
        ),
        name="pick_rows",
    )(pos, rows)


def mix_kernel(pos_ref, weight_ref, rows_ref, out_ref):
    peers, _, cap, width = rows_ref.shape
    spreads = [
        jnp.where(slot_hits(pos_ref[p, 0], cap), weight_ref[p, 0], 0.0).astype(jnp.bfloat16)
        for p in range(peers)
    ]
    across = (((0,), (0,)), ((), ()))
    if cap % 16 == 0:
        total = lax.dot_general(
            jnp.concatenate(spreads, axis=0),
            rows_ref[:, 0].reshape(peers * cap, width),
            across,
            preferred_element_type=jnp.float32,
        )
    else:
        total = jnp.zeros(out_ref.shape, jnp.float32)
        for p in range(peers):
            total += lax.dot_general(
                spreads[p], rows_ref[p, 0], across, preferred_element_type=jnp.float32
            )
    out_ref[...] = total.astype(out_ref.dtype)


def mix_rows(pos, weight, rows):
    peers, groups, _, tokens = pos.shape
    cap, width = rows.shape[2:]
    part = min(PART, width)
    return pl.pallas_call(
        mix_kernel,
        grid=(groups, width // part),
        in_specs=[
            pl.BlockSpec((peers, 1, 1, tokens), lambda g, w: (0, g, 0, 0)),
            pl.BlockSpec((peers, 1, 1, tokens), lambda g, w: (0, g, 0, 0)),
            pl.BlockSpec((peers, 1, cap, part), lambda g, w: (0, g, 0, w)),
        ],
        out_specs=pl.BlockSpec((tokens, part), lambda g, w: (g, w)),
        out_shape=jax.ShapeDtypeStruct((groups * tokens, width), rows.dtype),
        cost_estimate=pl.CostEstimate(
            flops=2 * peers * groups * cap * tokens * width,
            bytes_accessed=2 * width * groups * (tokens + peers * cap),
            transcendentals=0,
        ),
        name="mix_rows",
    )(pos, weight, rows)


def doc_kernel(query_ref, grad_ref, key_ref, value_ref, out_ref, dkey_ref, dvalue_ref):
    head = pl.program_id(1)
    doc_len, dim = query_ref.shape
    scale_val = dim ** (-0.5)
    block = min(ATT_BLOCK, doc_len)

    @pl.when(head == 0)
    def _():
        dkey_ref[...] = jnp.zeros_like(dkey_ref)
        dvalue_ref[...] = jnp.zeros_like(dvalue_ref)

    key_turned = key_ref[...].T
    columns = pl.ds(pl.multiple_of(head * dim, dim), dim)
    for at in range(0, doc_len, block):
        seen = at + block
        query = query_ref[at:seen, :]
        grad = grad_ref[at:seen, :]
        scores = lax.dot_general(
            key_ref[:seen, :],
            query,
            (((1,), (1,)), ((), ())),
            preferred_element_type=jnp.float32,
        )
        key_at = lax.broadcasted_iota(jnp.int32, (block, block), 0)
        query_at = lax.broadcasted_iota(jnp.int32, (block, block), 1)
        corner = jnp.where(key_at <= query_at, scores[at:, :], -jnp.inf)
        scores = jnp.concatenate([scores[:at, :], corner], axis=0) if at else corner
        top = jnp.max(scores, axis=0, keepdims=True)
        expo = jnp.exp2((scores - top) * (scale_val * LOG2_E))
        probs = expo * (1.0 / jnp.sum(expo, axis=0, keepdims=True))
        dprob = lax.dot_general(
            value_ref[:seen, :],
            grad,
            (((1,), (1,)), ((), ())),
            preferred_element_type=jnp.float32,
        )
        delta = jnp.sum(probs * dprob, axis=0, keepdims=True)
        dscore = (probs * (dprob - delta)).astype(jnp.bfloat16)
        dvalue_ref[:seen, :] += jnp.dot(
            probs.astype(jnp.bfloat16), grad, preferred_element_type=jnp.float32
        )
        dkey_ref[:seen, :] += jnp.dot(dscore, query, preferred_element_type=jnp.float32)
        turned = jnp.dot(key_turned[:, :seen], dscore, preferred_element_type=jnp.float32)
        out_ref[at:seen, columns] = (turned.T * scale_val).astype(out_ref.dtype)

    @pl.when(head == pl.num_programs(1) - 1)
    def _():
        heads = out_ref.shape[1] // dim - 2
        out_ref[:, heads * dim : (heads + 1) * dim] = (dkey_ref[...] * scale_val).astype(
            out_ref.dtype
        )
        out_ref[:, (heads + 1) * dim :] = dvalue_ref[...].astype(out_ref.dtype)


def attention_backward(queries, out_grad, key_head, value_head):
    rows, width = queries.shape
    dim = key_head.shape[1]
    docs, heads = rows // DOC, width // dim
    return pl.pallas_call(
        doc_kernel,
        grid=(docs, heads),
        in_specs=[
            pl.BlockSpec((DOC, dim), lambda d, h: (d, h)),
            pl.BlockSpec((DOC, dim), lambda d, h: (d, h)),
            pl.BlockSpec((DOC, dim), lambda d, h: (d, 0)),
            pl.BlockSpec((DOC, dim), lambda d, h: (d, 0)),
        ],
        out_specs=pl.BlockSpec((DOC, width + 2 * dim), lambda d, h: (d, 0)),
        out_shape=jax.ShapeDtypeStruct((rows, width + 2 * dim), queries.dtype),
        scratch_shapes=[pltpu.VMEM((DOC, dim), jnp.float32)] * 2,
        cost_estimate=pl.CostEstimate(
            flops=10 * docs * heads * DOC * DOC * dim,
            bytes_accessed=2 * rows * (3 * width + 4 * dim),
            transcendentals=docs * heads * DOC * DOC,
        ),
        name="doc_backward",
    )(queries, out_grad, key_head, value_head)


def send(block, axis, step):
    count = lax.axis_size(axis)
    return lax.ppermute(block, axis, [(i, i ^ step) for i in range(count)])


def gather_plane(block, turn):
    col_count, section_count = lax.axis_size("col"), lax.axis_size("section")
    got = [block] + [None] * (col_count - 1)
    for k in range(1, col_count):
        if k & (k - 1) == 0:
            got[k] = send(block, "col", k)
    for k in range(1, col_count):
        if got[k] is None:
            bits = [b for b in (1 << i for i in range(k.bit_length())) if k & b]
            first = bits[turn % len(bits)]
            got[k] = send(got[first], "col", k ^ first)
    every = list(got)
    for shift in range(1, section_count):
        perm = [(i, (i - shift) % section_count) for i in range(section_count)]
        every += [lax.ppermute(g, "section", perm) for g in got]
    return every


def body(
    queries,
    keys,
    values,
    out_grad,
    q_weight,
    k_weight,
    v_weight,
    resid_grad,
    moe_input,
    expert_ids,
    route_weights,
    w_gate_up,
    w_down,
):
    row_count = lax.axis_size("row")
    heads_here = queries.shape[1] // HEAD_DIM
    group_size = HEADS // KV_HEADS
    kv_index = lax.axis_index("row") * heads_here // group_size
    key_head = lax.dynamic_slice_in_dim(keys, kv_index * HEAD_DIM, HEAD_DIM, 1)
    value_head = lax.dynamic_slice_in_dim(values, kv_index * HEAD_DIM, HEAD_DIM, 1)
    wk_local = lax.dynamic_slice_in_dim(k_weight, kv_index * HEAD_DIM, HEAD_DIM, 1)
    wv_local = lax.dynamic_slice_in_dim(v_weight, kv_index * HEAD_DIM, HEAD_DIM, 1)
    wcat_local = jnp.concatenate([q_weight, wk_local, wv_local], axis=1)
    wcat_whole = lax.all_gather(wcat_local, "col", axis=0, tiled=True)
    section_count = lax.axis_size("section")
    col_count = lax.axis_size("col")
    peers = section_count * col_count
    n_experts = peers * row_count
    tok_rows = queries.shape[0]
    moe_rows = tok_rows // row_count
    model = q_weight.shape[0] * col_count
    capacity = max(2, 9 * moe_rows * TOPK // (8 * n_experts))
    span = model // CHUNKS

    gu_parts = [w_gate_up[0, c * span : (c + 1) * span] for c in range(CHUNKS)]
    dn_parts = [w_down[0, :, c * span : (c + 1) * span] for c in range(CHUNKS)]
    gu_all = [gather_plane(p, c % 2) for c, p in enumerate(gu_parts)]
    dn_all = [gather_plane(p, c % 2) for c, p in enumerate(dn_parts)]

    routes = jnp.concatenate([expert_ids.astype(jnp.float32), route_weights], axis=1)
    routes_line = lax.all_gather(routes, "row", axis=0, tiled=False)
    ids_line = routes_line[..., :TOPK].astype(jnp.int32)
    weights_line = routes_line[..., TOPK:]
    rows_line = lax.all_to_all(
        jnp.broadcast_to(moe_input[None], (row_count,) + moe_input.shape),
        "row",
        split_axis=0,
        concat_axis=0,
        tiled=True,
    )
    peer = jnp.arange(peers, dtype=jnp.int32)
    peer_section = lax.rem(lax.axis_index("section") + peer // col_count, section_count)
    peer_col = lax.axis_index("col") ^ (peer % col_count)
    peer_expert = (peer_section * row_count + lax.axis_index("row")) * col_count + peer_col
    named = ids_line[None] == peer_expert[:, None, None, None]
    hit = jnp.any(named, axis=-1)
    weight = jnp.sum(jnp.where(named, weights_line[None], 0.0), axis=-1)
    order = jnp.arange(moe_rows, dtype=jnp.int32)
    before = (order[:, None] < order[None, :]).astype(jnp.bfloat16)
    rank = lax.dot_general(
        hit.astype(jnp.bfloat16).reshape(peers * row_count, moe_rows),
        before,
        (((1,), (0,)), ((), ())),
        preferred_element_type=jnp.float32,
    ).reshape(peers, row_count, moe_rows)
    pos = jnp.where(hit, rank.astype(jnp.int32), -1)[:, :, None, :]
    weight = weight[:, :, None, :]

    ff = w_down.shape[1]
    per_peer = row_count * capacity
    rows_in = pick_rows(pos, rows_line, capacity).reshape(peers, per_peer, model)

    dqkv = attention_backward(queries, out_grad, key_head, value_head)

    gate_up = []
    for p in range(peers):
        total = None
        for c in range(CHUNKS):
            term = jnp.dot(
                rows_in[p, :, c * span : (c + 1) * span],
                gu_all[c][p],
                preferred_element_type=jnp.float32,
            )
            total = term if total is None else total + term
        gate_up.append(total)

    dhidden = [None] * peers
    for chunk in range(CHUNKS):
        lo, hi = chunk * span, (chunk + 1) * span
        term = lax.dot_general(
            dqkv,
            wcat_whole[lo:hi],
            (((1,), (1,)), ((), ())),
            preferred_element_type=jnp.float32,
        )
        head_grad = lax.psum_scatter(
            term.astype(jnp.bfloat16), "row", scatter_dimension=0, tiled=True
        ).astype(jnp.float32)
        layer_grad = head_grad + resid_grad[:, lo:hi].astype(jnp.float32)
        row_grad = layer_grad.astype(jnp.bfloat16)
        grads_line = lax.all_gather(row_grad, "row", axis=0, tiled=False)
        grads_in = pick_rows(pos, grads_line, capacity).reshape(peers, per_peer, span)
        for p in range(peers):
            piece = lax.dot_general(
                grads_in[p],
                dn_all[chunk][p],
                (((1,), (1,)), ((), ())),
                preferred_element_type=jnp.float32,
            )
            dhidden[p] = piece if dhidden[p] is None else dhidden[p] + piece

    dgate_up = []
    for p in range(peers):
        gate = gate_up[p][:, :ff]
        up_part = gate_up[p][:, ff:]
        sigm = jax.nn.sigmoid(gate)
        d_gate = dhidden[p] * up_part * sigm * (1.0 + gate * (1.0 - sigm))
        d_up = dhidden[p] * gate * sigm
        dgate_up.append(jnp.concatenate([d_gate, d_up], axis=1).astype(jnp.bfloat16))

    pieces = []
    for chunk in range(CHUNKS):
        back_rows = [
            lax.dot_general(
                dgate_up[p],
                gu_all[chunk][p],
                (((1,), (1,)), ((), ())),
                preferred_element_type=jnp.float32,
            ).astype(jnp.bfloat16)
            for p in range(peers)
        ]
        back = jnp.stack(back_rows).reshape(peers, row_count, capacity, span)
        mixed = mix_rows(pos, weight, back)
        pieces.append(lax.psum_scatter(mixed, "row", scatter_dimension=0, tiled=True))
    return jnp.concatenate(pieces, axis=1)


def solution(mesh):
    return jax.shard_map(
        body,
        mesh=mesh,
        in_specs=(
            P(("section", "col"), "row"),
            P(("section", "col"), None),
            P(("section", "col"), None),
            P(("section", "col"), "row"),
            P("col", "row"),
            P("col", None),
            P("col", None),
            P(("section", "row", "col"), None),
            P(("section", "row", "col"), None),
            P(("section", "row", "col"), None),
            P(("section", "row", "col"), None),
            P(("section", "row", "col"), None, None),
            P(("section", "row", "col"), None, None),
        ),
        out_specs=P(("section", "row", "col"), None),
        check_vma=False,
    )
```

```python
import functools

import jax
import jax.numpy as jnp
from jax import lax
from jax.experimental import pallas as pl
from jax.experimental.pallas import tpu as pltpu
from jax.sharding import PartitionSpec as P


HEADS = 32
KV_HEADS = 4
HEAD_DIM = 128
TOPK = 8
DOC = 1024
CHUNKS = 2
PART = 512
ATT_BLOCK = 256
LOG2_E = 1.4426950408889634


def slot_hits(pos, cap):
    slot = lax.broadcasted_iota(jnp.int32, (cap, pos.shape[1]), 0)
    return slot == pos


def pick_kernel(pos_ref, rows_ref, out_ref):
    peers, _, cap, width = out_ref.shape
    picks = [
        jnp.where(slot_hits(pos_ref[p, 0], cap), 1.0, 0.0).astype(jnp.bfloat16)
        for p in range(peers)
    ]
    if cap % 16 == 0:
        picked = jnp.dot(
            jnp.concatenate(picks, axis=0), rows_ref[0], preferred_element_type=jnp.float32
        ).astype(out_ref.dtype)
        out_ref[:, 0] = picked.reshape(peers, cap, width)
    else:
        for p in range(peers):
            picked = jnp.dot(picks[p], rows_ref[0], preferred_element_type=jnp.float32)
            out_ref[p, 0] = picked.astype(out_ref.dtype)


def pick_rows(pos, rows, cap):
    peers, groups, _, tokens = pos.shape
    width = rows.shape[2]
    part = min(PART, width)
    return pl.pallas_call(
        pick_kernel,
        grid=(groups, width // part),
        in_specs=[
            pl.BlockSpec((peers, 1, 1, tokens), lambda g, w: (0, g, 0, 0)),
            pl.BlockSpec((1, tokens, part), lambda g, w: (g, 0, w)),
        ],
        out_specs=pl.BlockSpec((peers, 1, cap, part), lambda g, w: (0, g, 0, w)),
        out_shape=jax.ShapeDtypeStruct((peers, groups, cap, width), rows.dtype),
        cost_estimate=pl.CostEstimate(
            flops=2 * peers * groups * cap * tokens * width,
            bytes_accessed=2 * width * groups * (tokens + peers * cap),
            transcendentals=0,
        ),
        name="pick_rows",
    )(pos, rows)


def mix_kernel(pos_ref, weight_ref, rows_ref, out_ref):
    peers, _, cap, width = rows_ref.shape
    spreads = [
        jnp.where(slot_hits(pos_ref[p, 0], cap), weight_ref[p, 0], 0.0).astype(jnp.bfloat16)
        for p in range(peers)
    ]
    across = (((0,), (0,)), ((), ()))
    if cap % 16 == 0:
        total = lax.dot_general(
            jnp.concatenate(spreads, axis=0),
            rows_ref[:, 0].reshape(peers * cap, width),
            across,
            preferred_element_type=jnp.float32,
        )
    else:
        total = jnp.zeros(out_ref.shape, jnp.float32)
        for p in range(peers):
            total += lax.dot_general(
                spreads[p], rows_ref[p, 0], across, preferred_element_type=jnp.float32
            )
    out_ref[...] = total.astype(out_ref.dtype)


def mix_placed(place_ref, pos_ref, weight_ref, rows_ref, out_ref):
    mix_kernel(pos_ref, weight_ref, rows_ref, out_ref)


def mix_rows(place, pos, weight, rows):
    peers, groups, _, tokens = pos.shape
    cap, width = rows.shape[2:]
    part = min(PART, width)
    return pl.pallas_call(
        mix_placed,
        grid_spec=pltpu.PrefetchScalarGridSpec(
            num_scalar_prefetch=1,
            grid=(groups, width // part),
            in_specs=[
                pl.BlockSpec((peers, 1, 1, tokens), lambda g, w, at: (0, g, 0, 0)),
                pl.BlockSpec((peers, 1, 1, tokens), lambda g, w, at: (0, g, 0, 0)),
                pl.BlockSpec((peers, 1, cap, part), lambda g, w, at: (0, g, 0, w)),
            ],
            out_specs=pl.BlockSpec((tokens, part), lambda g, w, at: (at[g], w)),
        ),
        out_shape=jax.ShapeDtypeStruct((groups * tokens, width), rows.dtype),
        cost_estimate=pl.CostEstimate(
            flops=2 * peers * groups * cap * tokens * width,
            bytes_accessed=2 * width * groups * (tokens + peers * cap),
            transcendentals=0,
        ),
        name="mix_rows",
    )(place, pos, weight, rows)


def doc_kernel(query_ref, grad_ref, key_ref, value_ref, out_ref, dkey_ref, dvalue_ref):
    head = pl.program_id(1)
    doc_len, dim = query_ref.shape
    scale_val = dim ** (-0.5)
    block = min(ATT_BLOCK, doc_len)

    @pl.when(head == 0)
    def _():
        dkey_ref[...] = jnp.zeros_like(dkey_ref)
        dvalue_ref[...] = jnp.zeros_like(dvalue_ref)

    key_turned = key_ref[...].T
    columns = pl.ds(pl.multiple_of(head * dim, dim), dim)
    for at in range(0, doc_len, block):
        seen = at + block
        query = query_ref[at:seen, :]
        grad = grad_ref[at:seen, :]
        scores = lax.dot_general(
            key_ref[:seen, :],
            query,
            (((1,), (1,)), ((), ())),
            preferred_element_type=jnp.float32,
        )
        key_at = lax.broadcasted_iota(jnp.int32, (block, block), 0)
        query_at = lax.broadcasted_iota(jnp.int32, (block, block), 1)
        corner = jnp.where(key_at <= query_at, scores[at:, :], -jnp.inf)
        scores = jnp.concatenate([scores[:at, :], corner], axis=0) if at else corner
        top = jnp.max(scores, axis=0, keepdims=True)
        expo = jnp.exp2((scores - top) * (scale_val * LOG2_E))
        probs = expo * (1.0 / jnp.sum(expo, axis=0, keepdims=True))
        dprob = lax.dot_general(
            value_ref[:seen, :],
            grad,
            (((1,), (1,)), ((), ())),
            preferred_element_type=jnp.float32,
        )
        delta = jnp.sum(probs * dprob, axis=0, keepdims=True)
        dscore = (probs * (dprob - delta)).astype(jnp.bfloat16)
        dvalue_ref[:seen, :] += jnp.dot(
            probs.astype(jnp.bfloat16), grad, preferred_element_type=jnp.float32
        )
        dkey_ref[:seen, :] += jnp.dot(dscore, query, preferred_element_type=jnp.float32)
        turned = jnp.dot(key_turned[:, :seen], dscore, preferred_element_type=jnp.float32)
        out_ref[at:seen, columns] = (turned.T * scale_val).astype(out_ref.dtype)

    @pl.when(head == pl.num_programs(1) - 1)
    def _():
        heads = out_ref.shape[1] // dim - 2
        out_ref[:, heads * dim : (heads + 1) * dim] = (dkey_ref[...] * scale_val).astype(
            out_ref.dtype
        )
        out_ref[:, (heads + 1) * dim :] = dvalue_ref[...].astype(out_ref.dtype)


def attention_backward(queries, out_grad, key_head, value_head, doc):
    width = queries.shape[1]
    dim = key_head.shape[1]
    heads = width // dim
    return pl.pallas_call(
        doc_kernel,
        grid=(1, heads),
        in_specs=[
            pl.BlockSpec((DOC, dim), lambda d, h: (doc, h)),
            pl.BlockSpec((DOC, dim), lambda d, h: (doc, h)),
            pl.BlockSpec((DOC, dim), lambda d, h: (doc, 0)),
            pl.BlockSpec((DOC, dim), lambda d, h: (doc, 0)),
        ],
        out_specs=pl.BlockSpec((DOC, width + 2 * dim), lambda d, h: (0, 0)),
        out_shape=jax.ShapeDtypeStruct((DOC, width + 2 * dim), queries.dtype),
        scratch_shapes=[pltpu.VMEM((DOC, dim), jnp.float32)] * 2,
        cost_estimate=pl.CostEstimate(
            flops=10 * heads * DOC * DOC * dim,
            bytes_accessed=2 * DOC * (3 * width + 4 * dim),
            transcendentals=heads * DOC * DOC,
        ),
        name="doc_backward",
    )(queries, out_grad, key_head, value_head)


def tail_kernel(peers, *refs):
    grads_ref, part_ref, gate_up_ref = refs[:3]
    dn_refs = refs[3 : 3 + peers]
    gu_refs = refs[3 + peers : 3 + 2 * peers]
    dgate_ref, back_ref, dn_buf, gu_buf, sems = refs[3 + 2 * peers :]
    p = pl.program_id(0)
    ff = dn_buf.shape[1]

    def fetch(k, slot):
        return (
            pltpu.make_async_copy(dn_refs[k], dn_buf.at[slot], sems.at[0, slot]),
            pltpu.make_async_copy(gu_refs[k], gu_buf.at[slot], sems.at[1, slot]),
        )

    for k in range(peers):
        if k == 0:

            @pl.when(p == 0)
            def _():
                for copy in fetch(0, 0):
                    copy.start()

        if k + 1 < peers:

            @pl.when(p == k)
            def _(k=k):
                for copy in fetch(k + 1, (k + 1) % 2):
                    copy.start()

    slot = lax.rem(p, 2)
    pltpu.make_async_copy(dn_refs[0], dn_buf.at[slot], sems.at[0, slot]).wait()
    dhidden = part_ref[0] + lax.dot_general(
        grads_ref[0], dn_buf[slot], (((1,), (1,)), ((), ())), preferred_element_type=jnp.float32
    )
    gate = gate_up_ref[0, :, :ff].astype(jnp.float32)
    up_part = gate_up_ref[0, :, ff:].astype(jnp.float32)
    sigm = 1.0 / (1.0 + jnp.exp(-gate))
    d_gate = dhidden * up_part * sigm * (1.0 + gate * (1.0 - sigm))
    d_up = dhidden * gate * sigm
    dgate_ref[0, :, :ff] = d_gate.astype(dgate_ref.dtype)
    dgate_ref[0, :, ff:] = d_up.astype(dgate_ref.dtype)
    pltpu.make_async_copy(gu_refs[0], gu_buf.at[slot], sems.at[1, slot]).wait()
    back_ref[0] = lax.dot_general(
        dgate_ref[0], gu_buf[slot], (((1,), (1,)), ((), ())), preferred_element_type=jnp.float32
    ).astype(back_ref.dtype)


def expert_tail(grads, part, gate_up, dn, gu):
    peers, rows, span = grads.shape
    ff = part.shape[2]
    block = lambda *shape: pl.BlockSpec((1,) + shape, lambda p: (p, 0, 0))
    return pl.pallas_call(
        functools.partial(tail_kernel, peers),
        grid=(peers,),
        in_specs=[block(rows, span), block(rows, ff), block(rows, 2 * ff)]
        + [pl.BlockSpec(memory_space=pl.ANY)] * (2 * peers),
        out_specs=[block(rows, 2 * ff), block(rows, span)],
        out_shape=[
            jax.ShapeDtypeStruct((peers, rows, 2 * ff), grads.dtype),
            jax.ShapeDtypeStruct((peers, rows, span), grads.dtype),
        ],
        scratch_shapes=[
            pltpu.VMEM((2, ff, span), grads.dtype),
            pltpu.VMEM((2, span, 2 * ff), grads.dtype),
            pltpu.SemaphoreType.DMA((2, 2)),
        ],
        cost_estimate=pl.CostEstimate(
            flops=6 * peers * rows * span * ff,
            bytes_accessed=peers * (rows * (4 * span + 20 * ff) + 6 * ff * span),
            transcendentals=peers * rows * ff,
        ),
        name="expert_tail",
    )(grads, part, gate_up, *dn, *gu)


def send(block, axis, step):
    count = lax.axis_size(axis)
    return lax.ppermute(block, axis, [(i, i ^ step) for i in range(count)])


def after(value, *others):
    return lax.optimization_barrier((value,) + others)[0]


def shift(block, axis, step):
    count = lax.axis_size(axis)
    pairs = [(i, i + step) for i in range(count) if 0 <= i + step < count]
    return lax.ppermute(block, axis, pairs)


def line_gather(block, axis, covers):
    count, me = lax.axis_size(axis), lax.axis_index(axis)
    if count > 4:
        whole = lax.all_gather(block, axis, axis=0, tiled=False)
        return jnp.take(whole, lax.rem(me + count - jnp.arange(count), count), axis=0)
    ups, downs = [block], [block]
    for hop in range(1, count):
        up, down = ups[-1], downs[-1]
        if hop > 1 and covers:
            up, down = lax.optimization_barrier((up, down) + tuple(covers[hop - 2]))[:2]
        ups.append(shift(up, axis, 1))
        downs.append(shift(down, axis, -1))
    blocks = [block]
    for k in range(1, count):
        blocks.append(jnp.where(me >= k, ups[k], downs[count - k]))
    return jnp.stack(blocks)


def spread_col(block):
    return {k: send(block, "col", k) for k in range(1, lax.axis_size("col")) if k & (k - 1) == 0}


def relay_col(got, turn, *others):
    for k in range(1, lax.axis_size("col")):
        if k not in got:
            bits = [b for b in (1 << i for i in range(k.bit_length())) if k & b]
            first = bits[turn % len(bits)]
            got[k] = send(after(got[first], *others), "col", k ^ first)


def swap_section(block):
    count = lax.axis_size("section")
    return [
        lax.ppermute(block, "section", [(i, (i - step) % count) for i in range(count)])
        for step in range(1, count)
    ]


def body(
    queries,
    keys,
    values,
    out_grad,
    q_weight,
    k_weight,
    v_weight,
    resid_grad,
    moe_input,
    expert_ids,
    route_weights,
    w_gate_up,
    w_down,
):
    row_count = lax.axis_size("row")
    heads_here = queries.shape[1] // HEAD_DIM
    group_size = HEADS // KV_HEADS
    kv_index = lax.axis_index("row") * heads_here // group_size
    key_head = lax.dynamic_slice_in_dim(keys, kv_index * HEAD_DIM, HEAD_DIM, 1)
    value_head = lax.dynamic_slice_in_dim(values, kv_index * HEAD_DIM, HEAD_DIM, 1)
    wk_local = lax.dynamic_slice_in_dim(k_weight, kv_index * HEAD_DIM, HEAD_DIM, 1)
    wv_local = lax.dynamic_slice_in_dim(v_weight, kv_index * HEAD_DIM, HEAD_DIM, 1)
    wcat_local = jnp.concatenate([q_weight, wk_local, wv_local], axis=1)
    wcat_whole = lax.all_gather(wcat_local, "col", axis=0, tiled=True)
    section_count = lax.axis_size("section")
    col_count = lax.axis_size("col")
    peers = section_count * col_count
    n_experts = peers * row_count
    tok_rows = queries.shape[0]
    moe_rows = tok_rows // row_count
    model = q_weight.shape[0] * col_count
    capacity = max(2, 9 * moe_rows * TOPK // (8 * n_experts))
    span = model // CHUNKS

    per_peer = row_count * capacity
    docs = tok_rows // DOC

    dqkv = []
    for d in range(docs):
        source_rows = queries if d == 0 else after(queries, dqkv[-1])
        dqkv.append(attention_backward(source_rows, out_grad, key_head, value_head, d))

    def project(chunk, *others):
        return jnp.concatenate(
            [
                lax.dot_general(
                    after(part, *others) if others else part,
                    wcat_whole[chunk * span : (chunk + 1) * span],
                    (((1,), (1,)), ((), ())),
                    preferred_element_type=jnp.float32,
                ).astype(jnp.bfloat16)
                for part in dqkv
            ],
            axis=0,
        )

    terms = []
    for chunk in range(CHUNKS):
        terms.append(project(chunk, *terms[-1:]))
    heads_sum = [lax.psum_scatter(t, "row", scatter_dimension=0, tiled=True) for t in terms]

    rows_line = line_gather(moe_input, "row", [(dqkv[0],), (dqkv[-1],), ()])

    gu_own = [w_gate_up[0, c * span : (c + 1) * span] for c in range(CHUNKS)]
    dn_own = [w_down[0, :, c * span : (c + 1) * span] for c in range(CHUNKS)]
    gu_got = [{0: after(g, dqkv[0])} for g in gu_own]
    dn_got = [{0: after(g, terms[-1])} for g in dn_own]
    for c in range(CHUNKS):
        gu_got[c].update(spread_col(gu_got[c][0]))
        dn_got[c].update(spread_col(dn_got[c][0]))

    me = lax.axis_index("row")
    source = lax.rem(me + row_count - jnp.arange(row_count, dtype=jnp.int32), row_count)
    routes = jnp.concatenate([expert_ids.astype(jnp.float32), route_weights], axis=1)
    routes = after(routes, terms[-1])
    routes_line = lax.all_gather(routes, "row", axis=0, tiled=False)
    routes_line = jnp.take(routes_line, source, axis=0)
    ids_line = routes_line[..., :TOPK].astype(jnp.int32)
    weights_line = routes_line[..., TOPK:]
    peer = jnp.arange(peers, dtype=jnp.int32)
    peer_section = lax.rem(lax.axis_index("section") + peer // col_count, section_count)
    peer_col = lax.axis_index("col") ^ (peer % col_count)
    peer_expert = (peer_section * row_count + me) * col_count + peer_col
    named = ids_line[None] == peer_expert[:, None, None, None]
    hit = jnp.any(named, axis=-1)
    weight = jnp.sum(jnp.where(named, weights_line[None], 0.0), axis=-1)
    order = jnp.arange(moe_rows, dtype=jnp.int32)
    before = (order[:, None] < order[None, :]).astype(jnp.bfloat16)
    rank = lax.dot_general(
        hit.astype(jnp.bfloat16).reshape(peers * row_count, moe_rows),
        before,
        (((1,), (0,)), ((), ())),
        preferred_element_type=jnp.float32,
    ).reshape(peers, row_count, moe_rows)
    pos = jnp.where(hit, rank.astype(jnp.int32), -1)[:, :, None, :]
    weight = weight[:, :, None, :]

    rows_in = pick_rows(pos, rows_line, capacity).reshape(peers, per_peer, model)

    def enter(p, weights, *others):
        total = None
        for c in range(CHUNKS):
            rows = rows_in[p, :, c * span : (c + 1) * span]
            term = jnp.dot(
                after(rows, *others) if others else rows,
                weights[c],
                preferred_element_type=jnp.float32,
            )
            total = term if total is None else total + term
        return total.astype(rows_in.dtype)

    def swap(got, k, *others):
        for c in range(CHUNKS):
            for step, block in enumerate(swap_section(after(got[c][k], *others) if others else got[c][k])):
                got[c][k + (step + 1) * col_count] = block

    def column(got, p):
        return [got[c][p] for c in range(CHUNKS)]

    direct = [k for k in range(1, col_count) if k & (k - 1) == 0]
    relayed = [k for k in range(1, col_count) if k not in direct]
    others = range(1, section_count)
    gate_up = {}
    swap(gu_got, 0)
    swap(dn_got, 0)
    for s in range(section_count):
        gate_up[s * col_count] = enter(s * col_count, column(gu_got, s * col_count))
    first = tuple(gate_up.values())
    for c in range(CHUNKS):
        relay_col(gu_got[c], c, *first)
    for k in direct:
        swap(gu_got, k, *first)
        gate_up[k] = enter(k, column(gu_got, k), *first)
    second = tuple(gate_up[k] for k in direct)

    def row_grad_of(chunk, *others):
        head = after(heads_sum[chunk], *others) if others else heads_sum[chunk]
        resid = resid_grad[:, chunk * span : (chunk + 1) * span]
        return (head.astype(jnp.float32) + resid.astype(jnp.float32)).astype(jnp.bfloat16)

    grads_line = line_gather(row_grad_of(0, rows_in), "row", [first, second, ()])
    grads_in = pick_rows(pos, grads_line, capacity).reshape(peers, per_peer, span)
    for c in range(CHUNKS):
        relay_col(dn_got[c], c, *second)
    for k in direct:
        swap(dn_got, k, *second)
    for k in relayed:
        swap(gu_got, k, grads_in)
        swap(dn_got, k, grads_in)

    def hidden(p, chunk, grads):
        return lax.dot_general(
            grads[p],
            dn_got[chunk][p],
            (((1,), (1,)), ((), ())),
            preferred_element_type=jnp.float32,
        )

    for k in direct:
        for s in others:
            gate_up[k + s * col_count] = enter(k + s * col_count, column(gu_got, k + s * col_count), *second)
    third = (grads_in,) + tuple(gate_up[k + s * col_count] for k in direct for s in others)
    early = [p for p in range(peers) if p % col_count not in relayed]
    dhidden = {p: hidden(p, 0, grads_in) for p in early}
    fourth = tuple(dhidden.values())
    later_line = line_gather(row_grad_of(1, grads_line), "row", [third, fourth, ()])
    for p in range(peers):
        if p not in early:
            gate_up[p] = enter(p, column(gu_got, p), *third)
            dhidden[p] = hidden(p, 0, grads_in)
    later_in = pick_rows(pos, later_line, capacity).reshape(peers, per_peer, span)

    dgate_up, back = expert_tail(
        later_in,
        jnp.stack([dhidden[p] for p in range(peers)]),
        jnp.stack([gate_up[p] for p in range(peers)]),
        [dn_got[1][p] for p in range(peers)],
        [gu_got[0][p] for p in range(peers)],
    )
    backs = [back]
    backs.append(
        jnp.stack(
            [
                lax.dot_general(
                    dgate_up[p],
                    gu_got[1][p],
                    (((1,), (1,)), ((), ())),
                    preferred_element_type=jnp.float32,
                ).astype(jnp.bfloat16)
                for p in range(peers)
            ]
        )
    )
    pieces = []
    for back in backs:
        mixed = mix_rows(source, pos, weight, back.reshape(peers, row_count, capacity, span))
        pieces.append(lax.psum_scatter(mixed, "row", scatter_dimension=0, tiled=True))
    return jnp.concatenate(pieces, axis=1)


def solution(mesh):
    return jax.shard_map(
        body,
        mesh=mesh,
        in_specs=(
            P(("section", "col"), "row"),
            P(("section", "col"), None),
            P(("section", "col"), None),
            P(("section", "col"), "row"),
            P("col", "row"),
            P("col", None),
            P("col", None),
            P(("section", "row", "col"), None),
            P(("section", "row", "col"), None),
            P(("section", "row", "col"), None),
            P(("section", "row", "col"), None),
            P(("section", "row", "col"), None, None),
            P(("section", "row", "col"), None, None),
        ),
        out_specs=P(("section", "row", "col"), None),
        check_vma=False,
    )
```

```python
import functools

import jax
import jax.numpy as jnp
from jax import lax
from jax.experimental import pallas as pl
from jax.experimental.pallas import tpu as pltpu
from jax.sharding import PartitionSpec as P


HEADS = 32
KV_HEADS = 4
HEAD_DIM = 128
TOPK = 8
DOC = 1024
CHUNKS = 2
PART = 512
ATT_BLOCK = 256
LOG2_E = 1.4426950408889634


def slot_hits(pos, cap):
    slot = lax.broadcasted_iota(jnp.int32, (cap, pos.shape[1]), 0)
    return slot == pos


def pick_kernel(pos_ref, rows_ref, out_ref):
    peers, _, cap, width = out_ref.shape
    picks = [
        jnp.where(slot_hits(pos_ref[p, 0], cap), 1.0, 0.0).astype(jnp.bfloat16)
        for p in range(peers)
    ]
    if cap % 16 == 0:
        picked = jnp.dot(
            jnp.concatenate(picks, axis=0), rows_ref[0], preferred_element_type=jnp.float32
        ).astype(out_ref.dtype)
        out_ref[:, 0] = picked.reshape(peers, cap, width)
    else:
        for p in range(peers):
            picked = jnp.dot(picks[p], rows_ref[0], preferred_element_type=jnp.float32)
            out_ref[p, 0] = picked.astype(out_ref.dtype)


def pick_rows(pos, rows, cap):
    peers, groups, _, tokens = pos.shape
    width = rows.shape[2]
    part = min(PART, width)
    return pl.pallas_call(
        pick_kernel,
        grid=(groups, width // part),
        in_specs=[
            pl.BlockSpec((peers, 1, 1, tokens), lambda g, w: (0, g, 0, 0)),
            pl.BlockSpec((1, tokens, part), lambda g, w: (g, 0, w)),
        ],
        out_specs=pl.BlockSpec((peers, 1, cap, part), lambda g, w: (0, g, 0, w)),
        out_shape=jax.ShapeDtypeStruct((peers, groups, cap, width), rows.dtype),
        cost_estimate=pl.CostEstimate(
            flops=2 * peers * groups * cap * tokens * width,
            bytes_accessed=2 * width * groups * (tokens + peers * cap),
            transcendentals=0,
        ),
        name="pick_rows",
    )(pos, rows)


def mix_kernel(pos_ref, weight_ref, rows_ref, out_ref):
    peers, _, cap, width = rows_ref.shape
    spreads = [
        jnp.where(slot_hits(pos_ref[p, 0], cap), weight_ref[p, 0], 0.0).astype(jnp.bfloat16)
        for p in range(peers)
    ]
    across = (((0,), (0,)), ((), ()))
    if cap % 16 == 0:
        total = lax.dot_general(
            jnp.concatenate(spreads, axis=0),
            rows_ref[:, 0].reshape(peers * cap, width),
            across,
            preferred_element_type=jnp.float32,
        )
    else:
        total = jnp.zeros(out_ref.shape, jnp.float32)
        for p in range(peers):
            total += lax.dot_general(
                spreads[p], rows_ref[p, 0], across, preferred_element_type=jnp.float32
            )
    out_ref[...] = total.astype(out_ref.dtype)


def mix_placed(place_ref, pos_ref, weight_ref, rows_ref, out_ref):
    mix_kernel(pos_ref, weight_ref, rows_ref, out_ref)


def mix_rows(place, pos, weight, rows):
    peers, groups, _, tokens = pos.shape
    cap, width = rows.shape[2:]
    part = min(PART, width)
    return pl.pallas_call(
        mix_placed,
        grid_spec=pltpu.PrefetchScalarGridSpec(
            num_scalar_prefetch=1,
            grid=(groups, width // part),
            in_specs=[
                pl.BlockSpec((peers, 1, 1, tokens), lambda g, w, at: (0, g, 0, 0)),
                pl.BlockSpec((peers, 1, 1, tokens), lambda g, w, at: (0, g, 0, 0)),
                pl.BlockSpec((peers, 1, cap, part), lambda g, w, at: (0, g, 0, w)),
            ],
            out_specs=pl.BlockSpec((tokens, part), lambda g, w, at: (at[g], w)),
        ),
        out_shape=jax.ShapeDtypeStruct((groups * tokens, width), rows.dtype),
        cost_estimate=pl.CostEstimate(
            flops=2 * peers * groups * cap * tokens * width,
            bytes_accessed=2 * width * groups * (tokens + peers * cap),
            transcendentals=0,
        ),
        name="mix_rows",
    )(place, pos, weight, rows)


def doc_kernel(query_ref, grad_ref, key_ref, value_ref, out_ref, dkey_ref, dvalue_ref):
    head = pl.program_id(1)
    doc_len, dim = query_ref.shape
    scale_val = dim ** (-0.5)
    block = min(ATT_BLOCK, doc_len)

    @pl.when(head == 0)
    def _():
        dkey_ref[...] = jnp.zeros_like(dkey_ref)
        dvalue_ref[...] = jnp.zeros_like(dvalue_ref)

    key_turned = key_ref[...].T
    columns = pl.ds(pl.multiple_of(head * dim, dim), dim)
    for at in range(0, doc_len, block):
        seen = at + block
        query = query_ref[at:seen, :]
        grad = grad_ref[at:seen, :]
        scores = lax.dot_general(
            key_ref[:seen, :],
            query,
            (((1,), (1,)), ((), ())),
            preferred_element_type=jnp.float32,
        )
        key_at = lax.broadcasted_iota(jnp.int32, (block, block), 0)
        query_at = lax.broadcasted_iota(jnp.int32, (block, block), 1)
        corner = jnp.where(key_at <= query_at, scores[at:, :], -jnp.inf)
        scores = jnp.concatenate([scores[:at, :], corner], axis=0) if at else corner
        top = jnp.max(scores, axis=0, keepdims=True)
        expo = jnp.exp2((scores - top) * (scale_val * LOG2_E))
        probs = expo * (1.0 / jnp.sum(expo, axis=0, keepdims=True))
        dprob = lax.dot_general(
            value_ref[:seen, :],
            grad,
            (((1,), (1,)), ((), ())),
            preferred_element_type=jnp.float32,
        )
        delta = jnp.sum(probs * dprob, axis=0, keepdims=True)
        dscore = (probs * (dprob - delta)).astype(jnp.bfloat16)
        dvalue_ref[:seen, :] += jnp.dot(
            probs.astype(jnp.bfloat16), grad, preferred_element_type=jnp.float32
        )
        dkey_ref[:seen, :] += jnp.dot(dscore, query, preferred_element_type=jnp.float32)
        turned = jnp.dot(key_turned[:, :seen], dscore, preferred_element_type=jnp.float32)
        out_ref[at:seen, columns] = (turned.T * scale_val).astype(out_ref.dtype)

    @pl.when(head == pl.num_programs(1) - 1)
    def _():
        heads = out_ref.shape[1] // dim - 2
        out_ref[:, heads * dim : (heads + 1) * dim] = (dkey_ref[...] * scale_val).astype(
            out_ref.dtype
        )
        out_ref[:, (heads + 1) * dim :] = dvalue_ref[...].astype(out_ref.dtype)


def attention_backward(queries, out_grad, key_head, value_head, doc):
    width = queries.shape[1]
    dim = key_head.shape[1]
    heads = width // dim
    return pl.pallas_call(
        doc_kernel,
        grid=(1, heads),
        in_specs=[
            pl.BlockSpec((DOC, dim), lambda d, h: (doc, h)),
            pl.BlockSpec((DOC, dim), lambda d, h: (doc, h)),
            pl.BlockSpec((DOC, dim), lambda d, h: (doc, 0)),
            pl.BlockSpec((DOC, dim), lambda d, h: (doc, 0)),
        ],
        out_specs=pl.BlockSpec((DOC, width + 2 * dim), lambda d, h: (0, 0)),
        out_shape=jax.ShapeDtypeStruct((DOC, width + 2 * dim), queries.dtype),
        scratch_shapes=[pltpu.VMEM((DOC, dim), jnp.float32)] * 2,
        cost_estimate=pl.CostEstimate(
            flops=10 * heads * DOC * DOC * dim,
            bytes_accessed=2 * DOC * (3 * width + 4 * dim),
            transcendentals=heads * DOC * DOC,
        ),
        name="doc_backward",
    )(queries, out_grad, key_head, value_head)


def tail_kernel(peers, *refs):
    grads_ref, part_ref, gate_up_ref = refs[:3]
    dn_refs = refs[3 : 3 + peers]
    gu_refs = refs[3 + peers : 3 + 2 * peers]
    dgate_ref, back_ref, dn_buf, gu_buf, sems = refs[3 + 2 * peers :]
    p = pl.program_id(0)
    ff = dn_buf.shape[1]

    span = dn_buf.shape[2]

    def fetch(k, slot):
        dn, gu = dn_refs[k], gu_refs[k]
        return (
            pltpu.make_async_copy(
                dn.at[:, pl.ds(dn.shape[1] - span, span)], dn_buf.at[slot], sems.at[0, slot]
            ),
            pltpu.make_async_copy(gu.at[pl.ds(0, span)], gu_buf.at[slot], sems.at[1, slot]),
        )

    for k in range(peers):
        if k == 0:

            @pl.when(p == 0)
            def _():
                for copy in fetch(0, 0):
                    copy.start()

        if k + 1 < peers:

            @pl.when(p == k)
            def _(k=k):
                for copy in fetch(k + 1, (k + 1) % 2):
                    copy.start()

    slot = lax.rem(p, 2)
    dn_copy, gu_copy = fetch(0, slot)
    dn_copy.wait()
    dhidden = part_ref[0] + lax.dot_general(
        grads_ref[0], dn_buf[slot], (((1,), (1,)), ((), ())), preferred_element_type=jnp.float32
    )
    gate = gate_up_ref[0, :, :ff].astype(jnp.float32)
    up_part = gate_up_ref[0, :, ff:].astype(jnp.float32)
    sigm = 1.0 / (1.0 + jnp.exp(-gate))
    d_gate = dhidden * up_part * sigm * (1.0 + gate * (1.0 - sigm))
    d_up = dhidden * gate * sigm
    dgate_ref[0, :, :ff] = d_gate.astype(dgate_ref.dtype)
    dgate_ref[0, :, ff:] = d_up.astype(dgate_ref.dtype)
    gu_copy.wait()
    back_ref[0] = lax.dot_general(
        dgate_ref[0], gu_buf[slot], (((1,), (1,)), ((), ())), preferred_element_type=jnp.float32
    ).astype(back_ref.dtype)


def expert_tail(grads, part, gate_up, dn, gu):
    peers, rows, span = grads.shape
    ff = part.shape[2]
    block = lambda *shape: pl.BlockSpec((1,) + shape, lambda p: (p, 0, 0))
    return pl.pallas_call(
        functools.partial(tail_kernel, peers),
        grid=(peers,),
        in_specs=[block(rows, span), block(rows, ff), block(rows, 2 * ff)]
        + [pl.BlockSpec(memory_space=pl.ANY)] * (2 * peers),
        out_specs=[block(rows, 2 * ff), block(rows, span)],
        out_shape=[
            jax.ShapeDtypeStruct((peers, rows, 2 * ff), grads.dtype),
            jax.ShapeDtypeStruct((peers, rows, span), grads.dtype),
        ],
        scratch_shapes=[
            pltpu.VMEM((2, ff, span), grads.dtype),
            pltpu.VMEM((2, span, 2 * ff), grads.dtype),
            pltpu.SemaphoreType.DMA((2, 2)),
        ],
        cost_estimate=pl.CostEstimate(
            flops=6 * peers * rows * span * ff,
            bytes_accessed=peers * (rows * (4 * span + 20 * ff) + 6 * ff * span),
            transcendentals=peers * rows * ff,
        ),
        name="expert_tail",
    )(grads, part, gate_up, *dn, *gu)


def send(block, axis, step):
    count = lax.axis_size(axis)
    return lax.ppermute(block, axis, [(i, i ^ step) for i in range(count)])


def after(value, *others):
    return lax.optimization_barrier((value,) + others)[0]


def shift(block, axis, step):
    count = lax.axis_size(axis)
    pairs = [(i, i + step) for i in range(count) if 0 <= i + step < count]
    return lax.ppermute(block, axis, pairs)


def line_gather(block, axis, covers):
    count, me = lax.axis_size(axis), lax.axis_index(axis)
    if count > 4:
        whole = lax.all_gather(block, axis, axis=0, tiled=False)
        return jnp.take(whole, lax.rem(me + count - jnp.arange(count), count), axis=0)
    ups, downs = [block], [block]
    for hop in range(1, count):
        up, down = ups[-1], downs[-1]
        if hop > 1 and covers:
            up, down = lax.optimization_barrier((up, down) + tuple(covers[hop - 2]))[:2]
        ups.append(shift(up, axis, 1))
        downs.append(shift(down, axis, -1))
    blocks = [block]
    for k in range(1, count):
        blocks.append(jnp.where(me >= k, ups[k], downs[count - k]))
    return jnp.stack(blocks)


def swap_section(block):
    count = lax.axis_size("section")
    return [
        lax.ppermute(block, "section", [(i, (i - step) % count) for i in range(count)])
        for step in range(1, count)
    ]


def body(
    queries,
    keys,
    values,
    out_grad,
    q_weight,
    k_weight,
    v_weight,
    resid_grad,
    moe_input,
    expert_ids,
    route_weights,
    w_gate_up,
    w_down,
):
    row_count = lax.axis_size("row")
    heads_here = queries.shape[1] // HEAD_DIM
    group_size = HEADS // KV_HEADS
    kv_index = lax.axis_index("row") * heads_here // group_size
    key_head = lax.dynamic_slice_in_dim(keys, kv_index * HEAD_DIM, HEAD_DIM, 1)
    value_head = lax.dynamic_slice_in_dim(values, kv_index * HEAD_DIM, HEAD_DIM, 1)
    wk_local = lax.dynamic_slice_in_dim(k_weight, kv_index * HEAD_DIM, HEAD_DIM, 1)
    wv_local = lax.dynamic_slice_in_dim(v_weight, kv_index * HEAD_DIM, HEAD_DIM, 1)
    wcat_local = jnp.concatenate([q_weight, wk_local, wv_local], axis=1)
    wcat_whole = lax.all_gather(wcat_local, "col", axis=0, tiled=True)
    section_count = lax.axis_size("section")
    col_count = lax.axis_size("col")
    peers = section_count * col_count
    n_experts = peers * row_count
    tok_rows = queries.shape[0]
    moe_rows = tok_rows // row_count
    model = q_weight.shape[0] * col_count
    capacity = max(2, 9 * moe_rows * TOPK // (8 * n_experts))
    span = model // CHUNKS

    per_peer = row_count * capacity
    docs = tok_rows // DOC

    dqkv = []
    for d in range(docs):
        source_rows = queries if d == 0 else after(queries, dqkv[-1])
        dqkv.append(attention_backward(source_rows, out_grad, key_head, value_head, d))

    def project(chunk, *others):
        return jnp.concatenate(
            [
                lax.dot_general(
                    after(part, *others) if others else part,
                    wcat_whole[chunk * span : (chunk + 1) * span],
                    (((1,), (1,)), ((), ())),
                    preferred_element_type=jnp.float32,
                ).astype(jnp.bfloat16)
                for part in dqkv
            ],
            axis=0,
        )

    terms = []
    for chunk in range(CHUNKS):
        terms.append(project(chunk, *terms[-1:]))
    heads_sum = [lax.psum_scatter(t, "row", scatter_dimension=0, tiled=True) for t in terms]

    me = lax.axis_index("row")
    source = lax.rem(me + row_count - jnp.arange(row_count, dtype=jnp.int32), row_count)
    routes = jnp.concatenate([expert_ids.astype(jnp.float32), route_weights], axis=1)
    came = [routes]
    for k in range(1, row_count):
        pairs = [(r, (r + k) % row_count) for r in range(row_count)]
        came.append(lax.ppermute(routes, "row", pairs))
    routes_line = jnp.stack(came)
    routes_line = after(routes_line, terms[-1])
    ids_line = routes_line[..., :TOPK].astype(jnp.int32)
    weights_line = routes_line[..., TOPK:]
    peer = jnp.arange(peers, dtype=jnp.int32)
    peer_section = lax.rem(lax.axis_index("section") + peer // col_count, section_count)
    peer_col = lax.axis_index("col") ^ (peer % col_count)
    peer_expert = (peer_section * row_count + me) * col_count + peer_col
    named = ids_line[None] == peer_expert[:, None, None, None]
    hit = jnp.any(named, axis=-1)
    weight = jnp.sum(jnp.where(named, weights_line[None], 0.0), axis=-1)
    order = jnp.arange(moe_rows, dtype=jnp.int32)
    before = (order[:, None] < order[None, :]).astype(jnp.bfloat16)
    rank = lax.dot_general(
        hit.astype(jnp.bfloat16).reshape(peers * row_count, moe_rows),
        before,
        (((1,), (0,)), ((), ())),
        preferred_element_type=jnp.float32,
    ).reshape(peers, row_count, moe_rows)
    pos = jnp.where(hit, rank.astype(jnp.int32), -1)[:, :, None, :]
    weight = weight[:, :, None, :]

    def row_grad_of(chunk, *others):
        head = after(heads_sum[chunk], *others) if others else heads_sum[chunk]
        resid = resid_grad[:, chunk * span : (chunk + 1) * span]
        return (head.astype(jnp.float32) + resid.astype(jnp.float32)).astype(jnp.bfloat16)

    rows_line = line_gather(moe_input, "row", [(dqkv[-1],), (terms[-1],), ()])
    row_grad = row_grad_of(0)

    col_bits = [k for k in range(1, col_count) if k & (k - 1) == 0]
    mixed_bits = [k for k in range(1, col_count) if k not in col_bits]
    gu, dn = {}, {}

    def swap(got, k, *others):
        blocks = got[k] if isinstance(got[k], list) else [got[k]]
        moved = [swap_section(after(b, *others) if others else b) for b in blocks]
        for step in range(section_count - 1):
            pieces = [m[step] for m in moved]
            got[k + (step + 1) * col_count] = pieces if isinstance(got[k], list) else pieces[0]

    def direct(got):
        for k in col_bits:
            got[k] = send(got[0], "col", k)

    def relay(got, cut, *others):
        for k in mixed_bits:
            bits = [b for b in col_bits if k & b]
            got[k] = []
            for c in range(CHUNKS):
                first = bits[c % len(bits)]
                block = got[first] if isinstance(got[first], list) else None
                block = block[c] if block else cut(got[first], c)
                got[k].append(send(after(block, *others), "col", k ^ first))

    def cut_gu(block, c):
        return block[c * span : (c + 1) * span]

    def cut_dn(block, c):
        return block[:, c * span : (c + 1) * span]

    gu[0] = after(w_gate_up, dqkv[0])[0]
    dn[0] = after(w_down, dqkv[0])[0]
    direct(gu)
    swap(gu, 0)
    swap(dn, 0)

    def enter(p, *others):
        rows = after(rows_in[p], *others) if others else rows_in[p]
        if isinstance(gu[p], list):
            total = sum(
                jnp.dot(cut_dn(rows, c), gu[p][c], preferred_element_type=jnp.float32)
                for c in range(CHUNKS)
            )
        else:
            total = jnp.dot(rows, gu[p], preferred_element_type=jnp.float32)
        return total.astype(rows_in.dtype)

    def hidden(p, chunk, grads):
        block = dn[p][chunk] if isinstance(dn[p], list) else cut_dn(dn[p], chunk)
        return lax.dot_general(
            grads[p], block, (((1,), (1,)), ((), ())), preferred_element_type=jnp.float32
        )

    own = [s * col_count for s in range(section_count)]
    near = [k + b for k in own for b in col_bits]
    far = [p for p in range(peers) if p not in own + near]

    grads_line = None
    rows_line = after(rows_line, row_grad)
    rows_in = pick_rows(pos, rows_line, capacity).reshape(peers, per_peer, model)
    grads_line = line_gather(row_grad, "row", [(row_grad,), (rows_in,), ()])

    relay(gu, cut_gu, row_grad)
    dn_ready = dict(dn)
    dn[0] = after(dn[0], row_grad)
    direct(dn)
    dn.update({p: dn_ready[p] for p in own})
    for k in col_bits:
        swap(gu, k, row_grad)

    gate_up, dhidden = {}, {}
    for p in own:
        gate_up[p] = enter(p)
    row_grad_b = row_grad_of(1, grads_line)
    grads_in = pick_rows(pos, grads_line, capacity).reshape(peers, per_peer, span)
    for p in near[: len(col_bits)]:
        gate_up[p] = enter(p, row_grad_b)
    stage_a = (grads_in,) + tuple(gate_up[p] for p in near[: len(col_bits)])
    for p in near[len(col_bits) :]:
        gate_up[p] = enter(p, *stage_a)
    for p in own:
        dhidden[p] = hidden(p, 0, grads_in)
    stage_b = tuple(gate_up[p] for p in near[len(col_bits) :]) + tuple(dhidden[p] for p in own)
    middle = tuple(gate_up[p] for p in near[len(col_bits) : len(col_bits) + 1])
    later_line = line_gather(row_grad_b, "row", [stage_a, middle, ()])
    relay(dn, cut_dn, *stage_b)
    for k in col_bits:
        swap(dn, k, *stage_b)
    for k in mixed_bits:
        swap(gu, k, *stage_b)
        swap(dn, k, *stage_b)
    for p in near:
        dhidden[p] = hidden(p, 0, grads_in)
    later_in = pick_rows(pos, later_line, capacity).reshape(peers, per_peer, span)
    for p in far:
        gate_up[p] = enter(p, *stage_b)
        dhidden[p] = hidden(p, 0, grads_in)

    def half(got, p, c):
        return got[p][c] if isinstance(got[p], list) else got[p]

    dgate_up, back = expert_tail(
        later_in,
        jnp.stack([dhidden[p] for p in range(peers)]),
        jnp.stack([gate_up[p] for p in range(peers)]),
        [half(dn, p, 1) for p in range(peers)],
        [half(gu, p, 0) for p in range(peers)],
    )
    place = (peers, row_count, capacity, span)
    mixed = [mix_rows(source, pos, weight, back.reshape(place))]
    dgate_up = after(dgate_up, mixed[0])
    back = jnp.stack(
        [
            lax.dot_general(
                dgate_up[p],
                gu[p][1] if isinstance(gu[p], list) else cut_gu(gu[p], 1),
                (((1,), (1,)), ((), ())),
                preferred_element_type=jnp.float32,
            ).astype(jnp.bfloat16)
            for p in range(peers)
        ]
    )
    mixed.append(mix_rows(source, pos, weight, back.reshape(place)))
    return jnp.concatenate(
        [lax.psum_scatter(m, "row", scatter_dimension=0, tiled=True) for m in mixed], axis=1
    )


def solution(mesh):
    return jax.shard_map(
        body,
        mesh=mesh,
        in_specs=(
            P(("section", "col"), "row"),
            P(("section", "col"), None),
            P(("section", "col"), None),
            P(("section", "col"), "row"),
            P("col", "row"),
            P("col", None),
            P("col", None),
            P(("section", "row", "col"), None),
            P(("section", "row", "col"), None),
            P(("section", "row", "col"), None),
            P(("section", "row", "col"), None),
            P(("section", "row", "col"), None, None),
            P(("section", "row", "col"), None, None),
        ),
        out_specs=P(("section", "row", "col"), None),
        check_vma=False,
    )
```

```python
import functools

import jax
import jax.numpy as jnp
from jax import lax
from jax.experimental import pallas as pl
from jax.experimental.pallas import tpu as pltpu
from jax.sharding import PartitionSpec as P


HEADS = 32
KV_HEADS = 4
HEAD_DIM = 128
TOPK = 8
DOC = 1024
CHUNKS = 2
PART = 512
ATT_BLOCK = 256
LOG2_E = 1.4426950408889634


def slot_hits(pos, cap):
    slot = lax.broadcasted_iota(jnp.int32, (cap, pos.shape[1]), 0)
    return slot == pos


def pick_kernel(pos_ref, rows_ref, out_ref):
    peers, _, cap, width = out_ref.shape
    picks = [
        jnp.where(slot_hits(pos_ref[p, 0], cap), 1.0, 0.0).astype(jnp.bfloat16)
        for p in range(peers)
    ]
    if cap % 16 == 0:
        picked = jnp.dot(
            jnp.concatenate(picks, axis=0), rows_ref[0], preferred_element_type=jnp.float32
        ).astype(out_ref.dtype)
        out_ref[:, 0] = picked.reshape(peers, cap, width)
    else:
        for p in range(peers):
            picked = jnp.dot(picks[p], rows_ref[0], preferred_element_type=jnp.float32)
            out_ref[p, 0] = picked.astype(out_ref.dtype)


def pick_placed(place_ref, pos_ref, rows_ref, out_ref):
    pick_kernel(pos_ref, rows_ref, out_ref)


def pick_rows(place, pos, rows, cap):
    peers, groups, _, tokens = pos.shape
    width = rows.shape[2]
    part = min(PART, width)
    return pl.pallas_call(
        pick_placed,
        grid_spec=pltpu.PrefetchScalarGridSpec(
            num_scalar_prefetch=1,
            grid=(groups, width // part),
            in_specs=[
                pl.BlockSpec((peers, 1, 1, tokens), lambda g, w, at: (0, at[g], 0, 0)),
                pl.BlockSpec((1, tokens, part), lambda g, w, at: (g, 0, w)),
            ],
            out_specs=pl.BlockSpec((peers, 1, cap, part), lambda g, w, at: (0, at[g], 0, w)),
        ),
        out_shape=jax.ShapeDtypeStruct((peers, groups, cap, width), rows.dtype),
        cost_estimate=pl.CostEstimate(
            flops=2 * peers * groups * cap * tokens * width,
            bytes_accessed=2 * width * groups * (tokens + peers * cap),
            transcendentals=0,
        ),
        name="pick_rows",
    )(place, pos, rows)


def mix_kernel(pos_ref, weight_ref, rows_ref, out_ref):
    peers, _, cap, width = rows_ref.shape
    spreads = [
        jnp.where(slot_hits(pos_ref[p, 0], cap), weight_ref[p, 0], 0.0).astype(jnp.bfloat16)
        for p in range(peers)
    ]
    across = (((0,), (0,)), ((), ()))
    if cap % 16 == 0:
        total = lax.dot_general(
            jnp.concatenate(spreads, axis=0),
            rows_ref[:, 0].reshape(peers * cap, width),
            across,
            preferred_element_type=jnp.float32,
        )
    else:
        total = jnp.zeros(out_ref.shape, jnp.float32)
        for p in range(peers):
            total += lax.dot_general(
                spreads[p], rows_ref[p, 0], across, preferred_element_type=jnp.float32
            )
    out_ref[...] = total.astype(out_ref.dtype)


def mix_rows(pos, weight, rows):
    peers, groups, _, tokens = pos.shape
    cap, width = rows.shape[2:]
    part = min(PART, width)
    return pl.pallas_call(
        mix_kernel,
        grid=(groups, width // part),
        in_specs=[
            pl.BlockSpec((peers, 1, 1, tokens), lambda g, w: (0, g, 0, 0)),
            pl.BlockSpec((peers, 1, 1, tokens), lambda g, w: (0, g, 0, 0)),
            pl.BlockSpec((peers, 1, cap, part), lambda g, w: (0, g, 0, w)),
        ],
        out_specs=pl.BlockSpec((tokens, part), lambda g, w: (g, w)),
        out_shape=jax.ShapeDtypeStruct((groups * tokens, width), rows.dtype),
        cost_estimate=pl.CostEstimate(
            flops=2 * peers * groups * cap * tokens * width,
            bytes_accessed=2 * width * groups * (tokens + peers * cap),
            transcendentals=0,
        ),
        name="mix_rows",
    )(pos, weight, rows)


def doc_kernel(query_ref, grad_ref, key_ref, value_ref, out_ref, dkey_ref, dvalue_ref):
    head = pl.program_id(1)
    doc_len, dim = query_ref.shape
    scale_val = dim ** (-0.5)
    block = min(ATT_BLOCK, doc_len)

    @pl.when(head == 0)
    def _():
        dkey_ref[...] = jnp.zeros_like(dkey_ref)
        dvalue_ref[...] = jnp.zeros_like(dvalue_ref)

    key_turned = key_ref[...].T
    columns = pl.ds(pl.multiple_of(head * dim, dim), dim)
    for at in range(0, doc_len, block):
        seen = at + block
        query = query_ref[at:seen, :]
        grad = grad_ref[at:seen, :]
        scores = lax.dot_general(
            key_ref[:seen, :],
            query,
            (((1,), (1,)), ((), ())),
            preferred_element_type=jnp.float32,
        )
        key_at = lax.broadcasted_iota(jnp.int32, (block, block), 0)
        query_at = lax.broadcasted_iota(jnp.int32, (block, block), 1)
        corner = jnp.where(key_at <= query_at, scores[at:, :], -jnp.inf)
        scores = jnp.concatenate([scores[:at, :], corner], axis=0) if at else corner
        top = jnp.max(scores, axis=0, keepdims=True)
        expo = jnp.exp2((scores - top) * (scale_val * LOG2_E))
        probs = expo * (1.0 / jnp.sum(expo, axis=0, keepdims=True))
        dprob = lax.dot_general(
            value_ref[:seen, :],
            grad,
            (((1,), (1,)), ((), ())),
            preferred_element_type=jnp.float32,
        )
        delta = jnp.sum(probs * dprob, axis=0, keepdims=True)
        dscore = (probs * (dprob - delta)).astype(jnp.bfloat16)
        dvalue_ref[:seen, :] += jnp.dot(
            probs.astype(jnp.bfloat16), grad, preferred_element_type=jnp.float32
        )
        dkey_ref[:seen, :] += jnp.dot(dscore, query, preferred_element_type=jnp.float32)
        turned = jnp.dot(key_turned[:, :seen], dscore, preferred_element_type=jnp.float32)
        out_ref[at:seen, columns] = (turned.T * scale_val).astype(out_ref.dtype)

    @pl.when(head == pl.num_programs(1) - 1)
    def _():
        heads = out_ref.shape[1] // dim - 2
        out_ref[:, heads * dim : (heads + 1) * dim] = (dkey_ref[...] * scale_val).astype(
            out_ref.dtype
        )
        out_ref[:, (heads + 1) * dim :] = dvalue_ref[...].astype(out_ref.dtype)


def attention_backward(queries, out_grad, key_head, value_head, doc):
    width = queries.shape[1]
    dim = key_head.shape[1]
    heads = width // dim
    return pl.pallas_call(
        doc_kernel,
        grid=(1, heads),
        in_specs=[
            pl.BlockSpec((DOC, dim), lambda d, h: (doc, h)),
            pl.BlockSpec((DOC, dim), lambda d, h: (doc, h)),
            pl.BlockSpec((DOC, dim), lambda d, h: (doc, 0)),
            pl.BlockSpec((DOC, dim), lambda d, h: (doc, 0)),
        ],
        out_specs=pl.BlockSpec((DOC, width + 2 * dim), lambda d, h: (0, 0)),
        out_shape=jax.ShapeDtypeStruct((DOC, width + 2 * dim), queries.dtype),
        scratch_shapes=[pltpu.VMEM((DOC, dim), jnp.float32)] * 2,
        cost_estimate=pl.CostEstimate(
            flops=10 * heads * DOC * DOC * dim,
            bytes_accessed=2 * DOC * (3 * width + 4 * dim),
            transcendentals=heads * DOC * DOC,
        ),
        name="doc_backward",
    )(queries, out_grad, key_head, value_head)


def tail_kernel(peers, *refs):
    grads_ref, part_ref, gate_up_ref = refs[:3]
    dn_refs = refs[3 : 3 + peers]
    gu_refs = refs[3 + peers : 3 + 2 * peers]
    dgate_ref, back_ref, dn_buf, gu_buf, sems = refs[3 + 2 * peers :]
    p = pl.program_id(0)
    ff = dn_buf.shape[1]

    span = dn_buf.shape[2]

    def fetch(k, slot):
        dn, gu = dn_refs[k], gu_refs[k]
        return (
            pltpu.make_async_copy(
                dn.at[:, pl.ds(dn.shape[1] - span, span)], dn_buf.at[slot], sems.at[0, slot]
            ),
            pltpu.make_async_copy(gu.at[pl.ds(0, span)], gu_buf.at[slot], sems.at[1, slot]),
        )

    for k in range(peers):
        if k == 0:

            @pl.when(p == 0)
            def _():
                for copy in fetch(0, 0):
                    copy.start()

        if k + 1 < peers:

            @pl.when(p == k)
            def _(k=k):
                for copy in fetch(k + 1, (k + 1) % 2):
                    copy.start()

    slot = lax.rem(p, 2)
    dn_copy, gu_copy = fetch(0, slot)
    dn_copy.wait()
    dhidden = part_ref[0] + lax.dot_general(
        grads_ref[0], dn_buf[slot], (((1,), (1,)), ((), ())), preferred_element_type=jnp.float32
    )
    gate = gate_up_ref[0, :, :ff].astype(jnp.float32)
    up_part = gate_up_ref[0, :, ff:].astype(jnp.float32)
    sigm = 1.0 / (1.0 + jnp.exp(-gate))
    d_gate = dhidden * up_part * sigm * (1.0 + gate * (1.0 - sigm))
    d_up = dhidden * gate * sigm
    dgate_ref[0, :, :ff] = d_gate.astype(dgate_ref.dtype)
    dgate_ref[0, :, ff:] = d_up.astype(dgate_ref.dtype)
    gu_copy.wait()
    back_ref[0] = lax.dot_general(
        dgate_ref[0], gu_buf[slot], (((1,), (1,)), ((), ())), preferred_element_type=jnp.float32
    ).astype(back_ref.dtype)


def expert_tail(grads, part, gate_up, dn, gu):
    peers, rows, span = grads.shape
    ff = part.shape[2]
    block = lambda *shape: pl.BlockSpec((1,) + shape, lambda p: (p, 0, 0))
    return pl.pallas_call(
        functools.partial(tail_kernel, peers),
        grid=(peers,),
        in_specs=[block(rows, span), block(rows, ff), block(rows, 2 * ff)]
        + [pl.BlockSpec(memory_space=pl.ANY)] * (2 * peers),
        out_specs=[block(rows, 2 * ff), block(rows, span)],
        out_shape=[
            jax.ShapeDtypeStruct((peers, rows, 2 * ff), grads.dtype),
            jax.ShapeDtypeStruct((peers, rows, span), grads.dtype),
        ],
        scratch_shapes=[
            pltpu.VMEM((2, ff, span), grads.dtype),
            pltpu.VMEM((2, span, 2 * ff), grads.dtype),
            pltpu.SemaphoreType.DMA((2, 2)),
        ],
        cost_estimate=pl.CostEstimate(
            flops=6 * peers * rows * span * ff,
            bytes_accessed=peers * (rows * (4 * span + 20 * ff) + 6 * ff * span),
            transcendentals=peers * rows * ff,
        ),
        name="expert_tail",
    )(grads, part, gate_up, *dn, *gu)


def send(block, axis, step):
    count = lax.axis_size(axis)
    return lax.ppermute(block, axis, [(i, i ^ step) for i in range(count)])


def after(value, *others):
    return lax.optimization_barrier((value,) + others)[0]


def shift(block, axis, step):
    count = lax.axis_size(axis)
    pairs = [(i, i + step) for i in range(count) if 0 <= i + step < count]
    return lax.ppermute(block, axis, pairs)


def line_order(axis):
    count, me = lax.axis_size(axis), lax.axis_index(axis)
    order = jnp.arange(count, dtype=jnp.int32)
    return order if count > 4 else lax.rem(me + count - order, count)


def line_gather(block, axis, covers):
    count, me = lax.axis_size(axis), lax.axis_index(axis)
    if count > 4:
        return lax.all_gather(block, axis, axis=0, tiled=False)
    ups, downs = [block], [block]
    for hop in range(1, count):
        up, down = ups[-1], downs[-1]
        if hop > 1 and covers:
            up, down = lax.optimization_barrier((up, down) + tuple(covers[hop - 2]))[:2]
        ups.append(shift(up, axis, 1))
        downs.append(shift(down, axis, -1))
    blocks = [block]
    for k in range(1, count):
        blocks.append(jnp.where(me >= k, ups[k], downs[count - k]))
    return jnp.stack(blocks)


def swap_section(block):
    count = lax.axis_size("section")
    return [
        lax.ppermute(block, "section", [(i, (i - step) % count) for i in range(count)])
        for step in range(1, count)
    ]


def body(
    queries,
    keys,
    values,
    out_grad,
    q_weight,
    k_weight,
    v_weight,
    resid_grad,
    moe_input,
    expert_ids,
    route_weights,
    w_gate_up,
    w_down,
):
    row_count = lax.axis_size("row")
    heads_here = queries.shape[1] // HEAD_DIM
    group_size = HEADS // KV_HEADS
    kv_index = lax.axis_index("row") * heads_here // group_size
    key_head = lax.dynamic_slice_in_dim(keys, kv_index * HEAD_DIM, HEAD_DIM, 1)
    value_head = lax.dynamic_slice_in_dim(values, kv_index * HEAD_DIM, HEAD_DIM, 1)
    wk_local = lax.dynamic_slice_in_dim(k_weight, kv_index * HEAD_DIM, HEAD_DIM, 1)
    wv_local = lax.dynamic_slice_in_dim(v_weight, kv_index * HEAD_DIM, HEAD_DIM, 1)
    wcat_local = jnp.concatenate([q_weight, wk_local, wv_local], axis=1)
    wcat_whole = lax.all_gather(wcat_local, "col", axis=0, tiled=True)
    section_count = lax.axis_size("section")
    col_count = lax.axis_size("col")
    peers = section_count * col_count
    n_experts = peers * row_count
    tok_rows = queries.shape[0]
    moe_rows = tok_rows // row_count
    model = q_weight.shape[0] * col_count
    capacity = max(2, 9 * moe_rows * TOPK // (8 * n_experts))
    span = model // CHUNKS

    per_peer = row_count * capacity
    docs = tok_rows // DOC

    dqkv = []
    for d in range(docs):
        source_rows = queries if d == 0 else after(queries, dqkv[-1])
        dqkv.append(attention_backward(source_rows, out_grad, key_head, value_head, d))

    me = lax.axis_index("row")
    straight = jnp.arange(row_count, dtype=jnp.int32)
    blocks = DOC // moe_rows

    def resid_part(chunk):
        return resid_grad[:, chunk * span : (chunk + 1) * span].astype(jnp.float32)

    def project(d, chunk, *others):
        return lax.dot_general(
            after(dqkv[d], *others) if others else dqkv[d],
            wcat_whole[chunk * span : (chunk + 1) * span],
            (((1,), (1,)), ((), ())),
            preferred_element_type=jnp.float32,
        )

    def own_part(d, chunk, *others):
        part = project(d, chunk, *others).reshape(blocks, moe_rows, span)
        mine = (d * blocks + jnp.arange(blocks) == me)[:, None, None]
        part = part + jnp.where(mine, resid_part(chunk)[None], 0.0)
        return part.reshape(DOC, span).astype(jnp.bfloat16)

    units = [(d, chunk) for chunk in range(CHUNKS) for d in range(docs)]
    line = row_count == 4 and len(units) == 4
    parts = []
    for d, chunk in units:
        if line:
            parts.append(own_part(d, chunk, *parts[-1:]))
        else:
            parts.append(project(d, chunk).astype(jnp.bfloat16))
    inner = jnp.logical_and(me > 0, me < row_count - 1)

    def phase(block, pairs):
        return lax.ppermute(block, "row", pairs)

    def add(x, y):
        return (x.astype(jnp.float32) + y.astype(jnp.float32)).astype(jnp.bfloat16)

    if line:
        came = [phase(p, [(0, 1), (3, 2)]) for p in parts]
    sums, crossed, fulls, ended = {}, {}, {}, {}

    def join(u, *others):
        sums[u] = add(after(parts[u], *others) if others else parts[u], came[u])
        crossed[u] = phase(sums[u], [(1, 2), (2, 1)])

    def meet(u, *others):
        fulls[u] = add(after(sums[u], *others) if others else sums[u], crossed[u])
        ended[u] = phase(fulls[u], [(1, 0), (2, 3)])

    def settle(chunk, *others):
        have = [u for u, (d, c) in enumerate(units) if c == chunk]
        if line:
            first = after(fulls[have[0]], *others) if others else fulls[have[0]]
            use = [first] + [fulls[u] for u in have[1:]]
            whole = jnp.concatenate(
                [jnp.where(inner, f, ended[u]) for f, u in zip(use, have)], axis=0
            )
            return whole.reshape(row_count, moe_rows, span)
        term = jnp.concatenate([parts[u] for u in have], axis=0)
        head = lax.psum_scatter(term, "row", scatter_dimension=0, tiled=True)
        grad = (head.astype(jnp.float32) + resid_part(chunk)).astype(jnp.bfloat16)
        return lax.all_gather(grad, "row", axis=0, tiled=False)

    def stage(kind, u, *others):
        if not line:
            return parts[u]
        kind(u, *others)
        return sums[u] if kind is join else fulls[u]

    routes = jnp.concatenate([expert_ids.astype(jnp.float32), route_weights], axis=1)
    came_routes = [routes]
    for k in range(1, row_count):
        pairs = [(r, (r + k) % row_count) for r in range(row_count)]
        came_routes.append(lax.ppermute(routes, "row", pairs))
    back_order = lax.rem(me + row_count - straight, row_count)
    routes_line = jnp.stack(came_routes)
    routes_line = after(routes_line, parts[-1])
    ids_line = routes_line[..., :TOPK].astype(jnp.int32)
    weights_line = routes_line[..., TOPK:]
    peer = jnp.arange(peers, dtype=jnp.int32)
    peer_section = lax.rem(lax.axis_index("section") + peer // col_count, section_count)
    peer_col = lax.axis_index("col") ^ (peer % col_count)
    peer_expert = (peer_section * row_count + me) * col_count + peer_col
    named = ids_line[None] == peer_expert[:, None, None, None]
    hit = jnp.any(named, axis=-1)
    weight = jnp.sum(jnp.where(named, weights_line[None], 0.0), axis=-1)
    order = jnp.arange(moe_rows, dtype=jnp.int32)
    before = (order[:, None] < order[None, :]).astype(jnp.bfloat16)
    rank = lax.dot_general(
        hit.astype(jnp.bfloat16).reshape(peers * row_count, moe_rows),
        before,
        (((1,), (0,)), ((), ())),
        preferred_element_type=jnp.float32,
    ).reshape(peers, row_count, moe_rows)
    pos = jnp.where(hit, rank.astype(jnp.int32), -1)
    turn = (straight[:, None] == back_order[None, :]).astype(jnp.float32)
    pos = jnp.einsum("rk,pkt->prt", turn, pos.astype(jnp.float32), precision="highest").astype(jnp.int32)
    weight = jnp.einsum("rk,pkt->prt", turn, weight, precision="highest")
    pos, weight = pos[:, :, None, :], weight[:, :, None, :]

    col_bits = [k for k in range(1, col_count) if k & (k - 1) == 0]
    mixed_bits = [k for k in range(1, col_count) if k not in col_bits]
    gu, dn = {}, {}

    def swap(got, k, *others):
        pieces = got[k] if isinstance(got[k], list) else [got[k]]
        moved = [swap_section(after(b, *others) if others else b) for b in pieces]
        for step in range(section_count - 1):
            there = [m[step] for m in moved]
            got[k + (step + 1) * col_count] = there if isinstance(got[k], list) else there[0]

    def direct(got, block):
        for k in col_bits:
            got[k] = send(block, "col", k)

    def relay(got, cut, *others):
        for k in mixed_bits:
            bits = [b for b in col_bits if k & b]
            got[k] = []
            for c in range(CHUNKS):
                first = bits[c % len(bits)]
                block = got[first] if isinstance(got[first], list) else None
                block = block[c] if block else cut(after(got[first], *others), c)
                got[k].append(send(block, "col", k ^ first))

    def cut_gu(block, c):
        return block[c * span : (c + 1) * span]

    def cut_dn(block, c):
        return block[:, c * span : (c + 1) * span]

    gu[0] = after(w_gate_up, dqkv[0])[0]
    dn[0] = after(w_down, dqkv[0])[0]
    direct(gu, gu[0])
    direct(dn, after(w_down, parts[-1])[0])
    swap(gu, 0)
    swap(dn, 0)

    joined = stage(join, 0)
    rows_line = line_gather(moe_input, "row", [(dqkv[-1],), (joined,), ()])
    stage(join, 1)
    met = stage(meet, 0)
    rows_line = after(rows_line, met)
    rows_in = pick_rows(line_order("row"), pos, rows_line, capacity)
    rows_in = rows_in.reshape(peers, per_peer, model)

    def enter(p, *others):
        rows = after(rows_in[p], *others) if others else rows_in[p]
        if isinstance(gu[p], list):
            total = sum(
                jnp.dot(cut_dn(rows, c), gu[p][c], preferred_element_type=jnp.float32)
                for c in range(CHUNKS)
            )
        else:
            total = jnp.dot(rows, gu[p], preferred_element_type=jnp.float32)
        return total.astype(rows_in.dtype)

    def hidden(p, chunk, grads, *others):
        rows = after(grads[p], *others) if others else grads[p]
        block = dn[p][chunk] if isinstance(dn[p], list) else cut_dn(dn[p], chunk)
        return lax.dot_general(
            rows, block, (((1,), (1,)), ((), ())), preferred_element_type=jnp.float32
        )

    own = [s * col_count for s in range(section_count)]
    near = [k + b for k in own for b in col_bits]
    near_a, near_b = near[: len(col_bits)], near[len(col_bits) :]
    far = [p for p in range(peers) if p not in own + near]
    gate_up, dhidden = {}, {}

    stage(join, 2, rows_in)
    met = stage(meet, 1, rows_in)
    for k in col_bits:
        swap(gu, k, rows_in)
    relay(gu, cut_gu, met)
    for p in own + near_a:
        gate_up[p] = enter(p, met)
    entered = tuple(gate_up[p] for p in own + near_a)
    stage(join, 3, *entered)
    met = stage(meet, 2, *entered)
    grads_line = settle(0, met)
    grads_in = pick_rows(straight, pos, grads_line, capacity).reshape(peers, per_peer, span)
    for k in col_bits:
        swap(dn, k, grads_in)
    for p in near_b:
        gate_up[p] = enter(p, grads_in)
    for p in own:
        dhidden[p] = hidden(p, 0, grads_in)
    ready = tuple(gate_up[p] for p in near_b) + tuple(dhidden[p] for p in own)
    met = stage(meet, 3, *ready)
    relay(dn, cut_dn, met)
    for p in near:
        dhidden[p] = hidden(p, 0, grads_in, met)
    done = tuple(dhidden[p] for p in near)
    for k in mixed_bits:
        swap(gu, k, *done)
        swap(dn, k, *done)
    for p in far:
        gate_up[p] = enter(p, *done)
        dhidden[p] = hidden(p, 0, grads_in, *done)
    later_line = settle(1, met)
    later_in = pick_rows(straight, pos, later_line, capacity).reshape(peers, per_peer, span)

    def half(got, p, c):
        return got[p][c] if isinstance(got[p], list) else got[p]

    dgate_up, back = expert_tail(
        later_in,
        jnp.stack([dhidden[p] for p in range(peers)]),
        jnp.stack([gate_up[p] for p in range(peers)]),
        [half(dn, p, 1) for p in range(peers)],
        [half(gu, p, 0) for p in range(peers)],
    )
    place = (peers, row_count, capacity, span)
    mixed = [mix_rows(pos, weight, back.reshape(place))]
    dgate_up = after(dgate_up, mixed[0])
    back = jnp.stack(
        [
            lax.dot_general(
                dgate_up[p],
                gu[p][1] if isinstance(gu[p], list) else cut_gu(gu[p], 1),
                (((1,), (1,)), ((), ())),
                preferred_element_type=jnp.float32,
            ).astype(jnp.bfloat16)
            for p in range(peers)
        ]
    )
    mixed.append(mix_rows(pos, weight, back.reshape(place)))
    pieces = []
    for m in mixed:
        pieces.append(lax.psum_scatter(m, "row", scatter_dimension=0, tiled=True))
    return jnp.concatenate(pieces, axis=1)


def solution(mesh):
    return jax.shard_map(
        body,
        mesh=mesh,
        in_specs=(
            P(("section", "col"), "row"),
            P(("section", "col"), None),
            P(("section", "col"), None),
            P(("section", "col"), "row"),
            P("col", "row"),
            P("col", None),
            P("col", None),
            P(("section", "row", "col"), None),
            P(("section", "row", "col"), None),
            P(("section", "row", "col"), None),
            P(("section", "row", "col"), None),
            P(("section", "row", "col"), None, None),
            P(("section", "row", "col"), None, None),
        ),
        out_specs=P(("section", "row", "col"), None),
        check_vma=False,
    )
```

```python
import functools

import jax
import jax.numpy as jnp
from jax import lax
from jax.experimental import pallas as pl
from jax.experimental.pallas import tpu as pltpu
from jax.sharding import PartitionSpec as P


HEADS = 32
KV_HEADS = 4
HEAD_DIM = 128
TOPK = 8
DOC = 1024
CHUNKS = 2
PART = 512
ATT_BLOCK = 256
LOG2_E = 1.4426950408889634


def slot_hits(pos, cap):
    slot = lax.broadcasted_iota(jnp.int32, (cap, pos.shape[1]), 0)
    return slot == pos


def pick_kernel(pos_ref, rows_ref, out_ref):
    peers, _, cap, width = out_ref.shape
    picks = [
        jnp.where(slot_hits(pos_ref[p, 0], cap), 1.0, 0.0).astype(jnp.bfloat16)
        for p in range(peers)
    ]
    if cap % 16 == 0:
        picked = jnp.dot(
            jnp.concatenate(picks, axis=0), rows_ref[0], preferred_element_type=jnp.float32
        ).astype(out_ref.dtype)
        out_ref[:, 0] = picked.reshape(peers, cap, width)
    else:
        for p in range(peers):
            picked = jnp.dot(picks[p], rows_ref[0], preferred_element_type=jnp.float32)
            out_ref[p, 0] = picked.astype(out_ref.dtype)


def pick_placed(place_ref, pos_ref, rows_ref, out_ref):
    pick_kernel(pos_ref, rows_ref, out_ref)


def pick_rows(place, pos, rows, cap):
    peers, groups, _, tokens = pos.shape
    width = rows.shape[2]
    part = min(PART, width)
    return pl.pallas_call(
        pick_placed,
        grid_spec=pltpu.PrefetchScalarGridSpec(
            num_scalar_prefetch=1,
            grid=(groups, width // part),
            in_specs=[
                pl.BlockSpec((peers, 1, 1, tokens), lambda g, w, at: (0, at[g], 0, 0)),
                pl.BlockSpec((1, tokens, part), lambda g, w, at: (g, 0, w)),
            ],
            out_specs=pl.BlockSpec((peers, 1, cap, part), lambda g, w, at: (0, at[g], 0, w)),
        ),
        out_shape=jax.ShapeDtypeStruct((peers, groups, cap, width), rows.dtype),
        cost_estimate=pl.CostEstimate(
            flops=2 * peers * groups * cap * tokens * width,
            bytes_accessed=2 * width * groups * (tokens + peers * cap),
            transcendentals=0,
        ),
        name="pick_rows",
    )(place, pos, rows)


def mix_kernel(pos_ref, weight_ref, rows_ref, out_ref):
    peers, _, cap, width = rows_ref.shape
    spreads = [
        jnp.where(slot_hits(pos_ref[p, 0], cap), weight_ref[p, 0], 0.0).astype(jnp.bfloat16)
        for p in range(peers)
    ]
    across = (((0,), (0,)), ((), ()))
    if cap % 16 == 0:
        total = lax.dot_general(
            jnp.concatenate(spreads, axis=0),
            rows_ref[:, 0].reshape(peers * cap, width),
            across,
            preferred_element_type=jnp.float32,
        )
    else:
        total = jnp.zeros(out_ref.shape, jnp.float32)
        for p in range(peers):
            total += lax.dot_general(
                spreads[p], rows_ref[p, 0], across, preferred_element_type=jnp.float32
            )
    out_ref[...] = total.astype(out_ref.dtype)


def mix_rows(pos, weight, rows):
    peers, groups, _, tokens = pos.shape
    cap, width = rows.shape[2:]
    part = min(PART, width)
    return pl.pallas_call(
        mix_kernel,
        grid=(groups, width // part),
        in_specs=[
            pl.BlockSpec((peers, 1, 1, tokens), lambda g, w: (0, g, 0, 0)),
            pl.BlockSpec((peers, 1, 1, tokens), lambda g, w: (0, g, 0, 0)),
            pl.BlockSpec((peers, 1, cap, part), lambda g, w: (0, g, 0, w)),
        ],
        out_specs=pl.BlockSpec((tokens, part), lambda g, w: (g, w)),
        out_shape=jax.ShapeDtypeStruct((groups * tokens, width), rows.dtype),
        cost_estimate=pl.CostEstimate(
            flops=2 * peers * groups * cap * tokens * width,
            bytes_accessed=2 * width * groups * (tokens + peers * cap),
            transcendentals=0,
        ),
        name="mix_rows",
    )(pos, weight, rows)


def doc_kernel(query_ref, grad_ref, key_ref, value_ref, out_ref, dkey_ref, dvalue_ref):
    head = pl.program_id(1)
    doc_len, dim = query_ref.shape
    scale_val = dim ** (-0.5)
    block = min(ATT_BLOCK, doc_len)

    @pl.when(head == 0)
    def _():
        dkey_ref[...] = jnp.zeros_like(dkey_ref)
        dvalue_ref[...] = jnp.zeros_like(dvalue_ref)

    key_turned = key_ref[...].T
    columns = pl.ds(pl.multiple_of(head * dim, dim), dim)
    for at in range(0, doc_len, block):
        seen = at + block
        query = query_ref[at:seen, :]
        grad = grad_ref[at:seen, :]
        scores = lax.dot_general(
            key_ref[:seen, :],
            query,
            (((1,), (1,)), ((), ())),
            preferred_element_type=jnp.float32,
        )
        key_at = lax.broadcasted_iota(jnp.int32, (block, block), 0)
        query_at = lax.broadcasted_iota(jnp.int32, (block, block), 1)
        corner = jnp.where(key_at <= query_at, scores[at:, :], -jnp.inf)
        scores = jnp.concatenate([scores[:at, :], corner], axis=0) if at else corner
        top = jnp.max(scores, axis=0, keepdims=True)
        expo = jnp.exp2((scores - top) * (scale_val * LOG2_E))
        probs = expo * (1.0 / jnp.sum(expo, axis=0, keepdims=True))
        dprob = lax.dot_general(
            value_ref[:seen, :],
            grad,
            (((1,), (1,)), ((), ())),
            preferred_element_type=jnp.float32,
        )
        delta = jnp.sum(probs * dprob, axis=0, keepdims=True)
        dscore = (probs * (dprob - delta)).astype(jnp.bfloat16)
        dvalue_ref[:seen, :] += jnp.dot(
            probs.astype(jnp.bfloat16), grad, preferred_element_type=jnp.float32
        )
        dkey_ref[:seen, :] += jnp.dot(dscore, query, preferred_element_type=jnp.float32)
        turned = jnp.dot(key_turned[:, :seen], dscore, preferred_element_type=jnp.float32)
        out_ref[at:seen, columns] = (turned.T * scale_val).astype(out_ref.dtype)

    @pl.when(head == pl.num_programs(1) - 1)
    def _():
        heads = out_ref.shape[1] // dim - 2
        out_ref[:, heads * dim : (heads + 1) * dim] = (dkey_ref[...] * scale_val).astype(
            out_ref.dtype
        )
        out_ref[:, (heads + 1) * dim :] = dvalue_ref[...].astype(out_ref.dtype)


def attention_backward(queries, out_grad, key_head, value_head, doc):
    width = queries.shape[1]
    dim = key_head.shape[1]
    heads = width // dim
    return pl.pallas_call(
        doc_kernel,
        grid=(1, heads),
        in_specs=[
            pl.BlockSpec((DOC, dim), lambda d, h: (doc, h)),
            pl.BlockSpec((DOC, dim), lambda d, h: (doc, h)),
            pl.BlockSpec((DOC, dim), lambda d, h: (doc, 0)),
            pl.BlockSpec((DOC, dim), lambda d, h: (doc, 0)),
        ],
        out_specs=pl.BlockSpec((DOC, width + 2 * dim), lambda d, h: (0, 0)),
        out_shape=jax.ShapeDtypeStruct((DOC, width + 2 * dim), queries.dtype),
        scratch_shapes=[pltpu.VMEM((DOC, dim), jnp.float32)] * 2,
        cost_estimate=pl.CostEstimate(
            flops=10 * heads * DOC * DOC * dim,
            bytes_accessed=2 * DOC * (3 * width + 4 * dim),
            transcendentals=heads * DOC * DOC,
        ),
        name="doc_backward",
    )(queries, out_grad, key_head, value_head)


def tail_kernel(peers, *refs):
    grads_ref, part_ref, gate_up_ref = refs[:3]
    dn_refs = refs[3 : 3 + peers]
    gu_refs = refs[3 + peers : 3 + 2 * peers]
    dgate_ref, back_ref, dn_buf, gu_buf, sems = refs[3 + 2 * peers :]
    p = pl.program_id(0)
    ff = dn_buf.shape[1]

    span = dn_buf.shape[2]

    def fetch(k, slot):
        dn, gu = dn_refs[k], gu_refs[k]
        return (
            pltpu.make_async_copy(
                dn.at[:, pl.ds(dn.shape[1] - span, span)], dn_buf.at[slot], sems.at[0, slot]
            ),
            pltpu.make_async_copy(gu.at[pl.ds(0, span)], gu_buf.at[slot], sems.at[1, slot]),
        )

    for k in range(peers):
        if k == 0:

            @pl.when(p == 0)
            def _():
                for copy in fetch(0, 0):
                    copy.start()

        if k + 1 < peers:

            @pl.when(p == k)
            def _(k=k):
                for copy in fetch(k + 1, (k + 1) % 2):
                    copy.start()

    slot = lax.rem(p, 2)
    dn_copy, gu_copy = fetch(0, slot)
    dn_copy.wait()
    dhidden = part_ref[0] + lax.dot_general(
        grads_ref[0], dn_buf[slot], (((1,), (1,)), ((), ())), preferred_element_type=jnp.float32
    )
    gate = gate_up_ref[0, :, :ff].astype(jnp.float32)
    up_part = gate_up_ref[0, :, ff:].astype(jnp.float32)
    sigm = 1.0 / (1.0 + jnp.exp(-gate))
    d_gate = dhidden * up_part * sigm * (1.0 + gate * (1.0 - sigm))
    d_up = dhidden * gate * sigm
    dgate_ref[0, :, :ff] = d_gate.astype(dgate_ref.dtype)
    dgate_ref[0, :, ff:] = d_up.astype(dgate_ref.dtype)
    gu_copy.wait()
    back_ref[0] = lax.dot_general(
        dgate_ref[0], gu_buf[slot], (((1,), (1,)), ((), ())), preferred_element_type=jnp.float32
    ).astype(back_ref.dtype)


def expert_tail(grads, part, gate_up, dn, gu):
    peers, rows, span = grads.shape
    ff = part.shape[2]
    block = lambda *shape: pl.BlockSpec((1,) + shape, lambda p: (p, 0, 0))
    return pl.pallas_call(
        functools.partial(tail_kernel, peers),
        grid=(peers,),
        in_specs=[block(rows, span), block(rows, ff), block(rows, 2 * ff)]
        + [pl.BlockSpec(memory_space=pl.ANY)] * (2 * peers),
        out_specs=[block(rows, 2 * ff), block(rows, span)],
        out_shape=[
            jax.ShapeDtypeStruct((peers, rows, 2 * ff), grads.dtype),
            jax.ShapeDtypeStruct((peers, rows, span), grads.dtype),
        ],
        scratch_shapes=[
            pltpu.VMEM((2, ff, span), grads.dtype),
            pltpu.VMEM((2, span, 2 * ff), grads.dtype),
            pltpu.SemaphoreType.DMA((2, 2)),
        ],
        cost_estimate=pl.CostEstimate(
            flops=6 * peers * rows * span * ff,
            bytes_accessed=peers * (rows * (4 * span + 20 * ff) + 6 * ff * span),
            transcendentals=peers * rows * ff,
        ),
        name="expert_tail",
    )(grads, part, gate_up, *dn, *gu)


def send(block, axis, step):
    count = lax.axis_size(axis)
    return lax.ppermute(block, axis, [(i, i ^ step) for i in range(count)])


def after(value, *others):
    return lax.optimization_barrier((value,) + others)[0]


def shift(block, axis, step, hop):
    count = lax.axis_size(axis)
    pairs = [
        (i, i + step)
        for i in range(count)
        if 0 <= i + step < count and 0 <= i - step * (hop - 1) < count
    ]
    return lax.ppermute(block, axis, pairs)


def line_order(axis):
    count, me = lax.axis_size(axis), lax.axis_index(axis)
    order = jnp.arange(count, dtype=jnp.int32)
    return order if count > 4 else lax.rem(me + count - order, count)


def line_gather(block, axis, covers):
    count, me = lax.axis_size(axis), lax.axis_index(axis)
    if count > 4:
        return lax.all_gather(block, axis, axis=0, tiled=False)
    ups, downs = [block], [block]
    for hop in range(1, count):
        up, down = ups[-1], downs[-1]
        if hop > 1 and covers:
            up, down = lax.optimization_barrier((up, down) + tuple(covers[hop - 2]))[:2]
        ups.append(shift(up, axis, 1, hop))
        downs.append(shift(down, axis, -1, hop))
    blocks = [block]
    for k in range(1, count):
        blocks.append(jnp.where(me >= k, ups[k], downs[count - k]))
    return jnp.stack(blocks)


def swap_section(block):
    count = lax.axis_size("section")
    return [
        lax.ppermute(block, "section", [(i, (i - step) % count) for i in range(count)])
        for step in range(1, count)
    ]


def body(
    queries,
    keys,
    values,
    out_grad,
    q_weight,
    k_weight,
    v_weight,
    resid_grad,
    moe_input,
    expert_ids,
    route_weights,
    w_gate_up,
    w_down,
):
    row_count = lax.axis_size("row")
    heads_here = queries.shape[1] // HEAD_DIM
    group_size = HEADS // KV_HEADS
    kv_index = lax.axis_index("row") * heads_here // group_size
    key_head = lax.dynamic_slice_in_dim(keys, kv_index * HEAD_DIM, HEAD_DIM, 1)
    value_head = lax.dynamic_slice_in_dim(values, kv_index * HEAD_DIM, HEAD_DIM, 1)
    wk_local = lax.dynamic_slice_in_dim(k_weight, kv_index * HEAD_DIM, HEAD_DIM, 1)
    wv_local = lax.dynamic_slice_in_dim(v_weight, kv_index * HEAD_DIM, HEAD_DIM, 1)
    wcat_local = jnp.concatenate([q_weight, wk_local, wv_local], axis=1)
    wcat_whole = lax.all_gather(wcat_local, "col", axis=0, tiled=True)
    section_count = lax.axis_size("section")
    col_count = lax.axis_size("col")
    peers = section_count * col_count
    n_experts = peers * row_count
    tok_rows = queries.shape[0]
    moe_rows = tok_rows // row_count
    model = q_weight.shape[0] * col_count
    capacity = max(2, 9 * moe_rows * TOPK // (8 * n_experts))
    span = model // CHUNKS

    per_peer = row_count * capacity
    docs = tok_rows // DOC

    dqkv = []
    for d in range(docs):
        source_rows = queries if d == 0 else after(queries, dqkv[-1])
        dqkv.append(attention_backward(source_rows, out_grad, key_head, value_head, d))

    me = lax.axis_index("row")
    straight = jnp.arange(row_count, dtype=jnp.int32)
    blocks = DOC // moe_rows

    def resid_part(chunk):
        return resid_grad[:, chunk * span : (chunk + 1) * span].astype(jnp.float32)

    def project(d, chunk, *others):
        return lax.dot_general(
            after(dqkv[d], *others) if others else dqkv[d],
            wcat_whole[chunk * span : (chunk + 1) * span],
            (((1,), (1,)), ((), ())),
            preferred_element_type=jnp.float32,
        )

    def own_part(d, chunk, *others):
        part = project(d, chunk, *others).reshape(blocks, moe_rows, span)
        mine = (d * blocks + jnp.arange(blocks) == me)[:, None, None]
        part = part + jnp.where(mine, resid_part(chunk)[None], 0.0)
        return part.reshape(DOC, span).astype(jnp.bfloat16)

    units = [(d, chunk) for chunk in range(CHUNKS) for d in range(docs)]
    line = row_count == 4 and len(units) == 4
    parts = []
    for d, chunk in units:
        if line:
            parts.append(own_part(d, chunk, *parts[-1:]))
        else:
            parts.append(project(d, chunk).astype(jnp.bfloat16))
    inner = jnp.logical_and(me > 0, me < row_count - 1)

    def phase(block, pairs):
        return lax.ppermute(block, "row", pairs)

    def add(x, y):
        return (x.astype(jnp.float32) + y.astype(jnp.float32)).astype(jnp.bfloat16)

    if line:
        came = [phase(p, [(0, 1), (3, 2)]) for p in parts]
    sums, crossed, fulls, ended = {}, {}, {}, {}

    def join(u, *others):
        sums[u] = add(after(parts[u], *others) if others else parts[u], came[u])
        crossed[u] = phase(sums[u], [(1, 2), (2, 1)])

    def meet(u, *others):
        fulls[u] = add(after(sums[u], *others) if others else sums[u], crossed[u])
        ended[u] = phase(fulls[u], [(1, 0), (2, 3)])

    def settle(chunk, *others):
        have = [u for u, (d, c) in enumerate(units) if c == chunk]
        if line:
            first = after(fulls[have[0]], *others) if others else fulls[have[0]]
            use = [first] + [fulls[u] for u in have[1:]]
            whole = jnp.concatenate(
                [jnp.where(inner, f, ended[u]) for f, u in zip(use, have)], axis=0
            )
            return whole.reshape(row_count, moe_rows, span)
        term = jnp.concatenate([parts[u] for u in have], axis=0)
        head = lax.psum_scatter(term, "row", scatter_dimension=0, tiled=True)
        grad = (head.astype(jnp.float32) + resid_part(chunk)).astype(jnp.bfloat16)
        return lax.all_gather(grad, "row", axis=0, tiled=False)

    def stage(kind, u, *others):
        if not line:
            return parts[u]
        kind(u, *others)
        return sums[u] if kind is join else fulls[u]

    routes = jnp.concatenate([expert_ids.astype(jnp.float32), route_weights], axis=1)
    came_routes = [routes]
    for k in range(1, row_count):
        pairs = [(r, (r + k) % row_count) for r in range(row_count)]
        came_routes.append(lax.ppermute(routes, "row", pairs))
    back_order = lax.rem(me + row_count - straight, row_count)
    routes_line = jnp.stack(came_routes)
    routes_line = after(routes_line, parts[-1])
    ids_line = routes_line[..., :TOPK].astype(jnp.int32)
    weights_line = routes_line[..., TOPK:]
    peer = jnp.arange(peers, dtype=jnp.int32)
    peer_section = lax.rem(lax.axis_index("section") + peer // col_count, section_count)
    peer_col = lax.axis_index("col") ^ (peer % col_count)
    peer_expert = (peer_section * row_count + me) * col_count + peer_col
    named = ids_line[None] == peer_expert[:, None, None, None]
    hit = jnp.any(named, axis=-1)
    weight = jnp.sum(jnp.where(named, weights_line[None], 0.0), axis=-1)
    order = jnp.arange(moe_rows, dtype=jnp.int32)
    before = (order[:, None] < order[None, :]).astype(jnp.bfloat16)
    rank = lax.dot_general(
        hit.astype(jnp.bfloat16).reshape(peers * row_count, moe_rows),
        before,
        (((1,), (0,)), ((), ())),
        preferred_element_type=jnp.float32,
    ).reshape(peers, row_count, moe_rows)
    pos = jnp.where(hit, rank.astype(jnp.int32), -1)
    turn = (straight[:, None] == back_order[None, :]).astype(jnp.float32)
    pos = jnp.einsum("rk,pkt->prt", turn, pos.astype(jnp.float32), precision="highest").astype(jnp.int32)
    weight = jnp.einsum("rk,pkt->prt", turn, weight, precision="highest")
    pos, weight = pos[:, :, None, :], weight[:, :, None, :]

    col_bits = [k for k in range(1, col_count) if k & (k - 1) == 0]
    mixed_bits = [k for k in range(1, col_count) if k not in col_bits]
    gu, dn = {}, {}

    def swap(got, k, *others):
        pieces = got[k] if isinstance(got[k], list) else [got[k]]
        moved = [swap_section(after(b, *others) if others else b) for b in pieces]
        for step in range(section_count - 1):
            there = [m[step] for m in moved]
            got[k + (step + 1) * col_count] = there if isinstance(got[k], list) else there[0]

    def direct(got, block):
        for k in col_bits:
            got[k] = send(block, "col", k)

    def relay(got, cut, *others):
        for k in mixed_bits:
            bits = [b for b in col_bits if k & b]
            got[k] = []
            for c in range(CHUNKS):
                first = bits[c % len(bits)]
                block = got[first] if isinstance(got[first], list) else None
                block = block[c] if block else cut(after(got[first], *others), c)
                got[k].append(send(block, "col", k ^ first))

    def cut_gu(block, c):
        return block[c * span : (c + 1) * span]

    def cut_dn(block, c):
        return block[:, c * span : (c + 1) * span]

    gu[0] = after(w_gate_up, dqkv[0])[0]
    dn[0] = after(w_down, dqkv[0])[0]
    direct(gu, gu[0])
    direct(dn, after(w_down, parts[-1])[0])
    swap(gu, 0)
    swap(dn, 0)

    joined = stage(join, 0)
    rows_line = line_gather(moe_input, "row", [(dqkv[-1],), (joined,), ()])
    stage(join, 1)
    met = stage(meet, 0)
    rows_line = after(rows_line, met)
    rows_in = pick_rows(line_order("row"), pos, rows_line, capacity)
    rows_in = rows_in.reshape(peers, per_peer, model)

    def enter(p, *others):
        rows = after(rows_in[p], *others) if others else rows_in[p]
        if isinstance(gu[p], list):
            total = sum(
                jnp.dot(cut_dn(rows, c), gu[p][c], preferred_element_type=jnp.float32)
                for c in range(CHUNKS)
            )
        else:
            total = jnp.dot(rows, gu[p], preferred_element_type=jnp.float32)
        return total.astype(rows_in.dtype)

    def hidden(p, chunk, grads, *others):
        rows = after(grads[p], *others) if others else grads[p]
        block = dn[p][chunk] if isinstance(dn[p], list) else cut_dn(dn[p], chunk)
        return lax.dot_general(
            rows, block, (((1,), (1,)), ((), ())), preferred_element_type=jnp.float32
        )

    own = [s * col_count for s in range(section_count)]
    near = [k + b for k in own for b in col_bits]
    near_a, near_b = near[: len(col_bits)], near[len(col_bits) :]
    far = [p for p in range(peers) if p not in own + near]
    gate_up, dhidden = {}, {}

    stage(join, 2, rows_in)
    met = stage(meet, 1, rows_in)
    for k in col_bits:
        swap(gu, k, rows_in)
    relay(gu, cut_gu, met)
    for p in own + near_a:
        gate_up[p] = enter(p, met)
    entered = tuple(gate_up[p] for p in own + near_a)
    stage(join, 3, *entered)
    met = stage(meet, 2, *entered)
    grads_line = settle(0, met)
    grads_in = pick_rows(straight, pos, grads_line, capacity).reshape(peers, per_peer, span)
    for k in col_bits:
        swap(dn, k, grads_in)
    for p in near_b:
        gate_up[p] = enter(p, grads_in)
    for p in own:
        dhidden[p] = hidden(p, 0, grads_in)
    ready = tuple(gate_up[p] for p in near_b) + tuple(dhidden[p] for p in own)
    met = stage(meet, 3, *ready)
    relay(dn, cut_dn, met)
    for p in near:
        dhidden[p] = hidden(p, 0, grads_in, met)
    done = tuple(dhidden[p] for p in near)
    for k in mixed_bits:
        swap(gu, k, *done)
        swap(dn, k, *done)
    for p in far:
        gate_up[p] = enter(p, *done)
        dhidden[p] = hidden(p, 0, grads_in, *done)
    later_line = settle(1, met)
    later_in = pick_rows(straight, pos, later_line, capacity).reshape(peers, per_peer, span)

    def half(got, p, c):
        return got[p][c] if isinstance(got[p], list) else got[p]

    dgate_up, back = expert_tail(
        later_in,
        jnp.stack([dhidden[p] for p in range(peers)]),
        jnp.stack([gate_up[p] for p in range(peers)]),
        [half(dn, p, 1) for p in range(peers)],
        [half(gu, p, 0) for p in range(peers)],
    )
    place = (peers, row_count, capacity, span)
    mixed = [mix_rows(pos, weight, back.reshape(place))]
    dgate_up = after(dgate_up, mixed[0])
    back = jnp.stack(
        [
            lax.dot_general(
                dgate_up[p],
                gu[p][1] if isinstance(gu[p], list) else cut_gu(gu[p], 1),
                (((1,), (1,)), ((), ())),
                preferred_element_type=jnp.float32,
            ).astype(jnp.bfloat16)
            for p in range(peers)
        ]
    )
    mixed.append(mix_rows(pos, weight, back.reshape(place)))
    pieces = []
    for m in mixed:
        pieces.append(lax.psum_scatter(m, "row", scatter_dimension=0, tiled=True))
    return jnp.concatenate(pieces, axis=1)


def solution(mesh):
    return jax.shard_map(
        body,
        mesh=mesh,
        in_specs=(
            P(("section", "col"), "row"),
            P(("section", "col"), None),
            P(("section", "col"), None),
            P(("section", "col"), "row"),
            P("col", "row"),
            P("col", None),
            P("col", None),
            P(("section", "row", "col"), None),
            P(("section", "row", "col"), None),
            P(("section", "row", "col"), None),
            P(("section", "row", "col"), None),
            P(("section", "row", "col"), None, None),
            P(("section", "row", "col"), None, None),
        ),
        out_specs=P(("section", "row", "col"), None),
        check_vma=False,
    )
```
